128 devices in a mesh: member: 8 (over z, y_lo), space: 16 (over x, y_hi, core).
Axes of the slice: x: 4, y: 4 (y_hi: 2, y_lo: 2; y = y_hi * 2 + y_lo), z: 4, core: 2. Of those that a mesh axis runs over, the one named last changes fastest.
Arguments:
- features: bfloat16 [8, 1024, 65536], P('member', None, 'space'), may hold values from -6 to 6
- up_weight: bfloat16 [1024, 1024], replicated, may hold values from -0.1875 to 0.1875
- out_weight: bfloat16 [1024, 100], replicated, may hold values from -0.1875 to 0.1875
- target: bfloat16 [100, 65536], P(None, 'space'), may hold values from -6 to 6
- area: float32 [65536], P('space'), may hold values from 0.1 to 1
Outputs:
- feature_grad: bfloat16 [8, 1024, 65536], P('member', None, 'space')
- up_grad: float32 [1024, 1024], P(('member', 'space'))
- out_grad: float32 [1024, 100], P(('member', 'space'))
The draws below stay inside these ranges and needn't reach their ends.
All inputs are finite; a program needn't handle non-finite values.
Results may differ from the reference program's by a relative error of at most 0.007.
Values sent between devices are 32-bit elements; how exact they have to be, the bound alone decides.
No kernel may reach another device: no remote copies, remote signals or barrier semaphores. Data moves between devices by JAX's collectives and lax.ppermute only.
A program may use at most 128 MiB of HBM per device.

```python
import math
import jax
import jax.numpy as jnp
from jax import lax

D = 1024
C = 100
MEMBERS = 8
CELLS = 65536


def spiked(values, stream_key, source, target, parts, factor):
    owner, partner = [(jnp.arange(values.shape[dim]) // (values.shape[dim] // parts)).reshape([-1 if axis == dim else 1 for axis in range(values.ndim)]) for dim in (source, target)]
    chosen = jax.random.permutation(stream_key, parts)[partner]
    strong = (owner == chosen) | (owner == (partner + parts // 2) % parts)
    return jnp.where(strong, factor * values, values)


def shard_levels(key, shape, split, smallest, high):
    def one(axis_at, shards_of):
        steps = jax.random.uniform(jax.random.fold_in(jax.random.fold_in(key, 6), axis_at), (shards_of,), jnp.float32, smallest / len(split), high / len(split))
        return jnp.repeat(jnp.exp(steps), shape[axis_at] // shards_of).reshape((-1,) + (1,) * (len(shape) - axis_at - 1))

    level = one(*split[0])
    for cut in split[1:]:
        level = level * one(*cut)
    return level


def noise(stream_key, shape, spread, bound, shards=(), held_as=jnp.bfloat16):
    result = jax.random.normal(stream_key, shape, jnp.float32) * spread
    if len(shards) > 0:
        result = shard_levels(stream_key, shape, shards, -0.22, 0.18) * result
    return jnp.clip(result, min=-bound, max=bound).astype(held_as)


def bell_draw_with(key, shape, width, limit, cuts, heavy, kind=jnp.bfloat16):
    drawn = width * jax.random.normal(key, shape, jnp.float32)
    if cuts:
        drawn = drawn * shard_levels(key, shape, cuts, -0.22, 0.18)
    return jnp.clip(spiked(drawn, jax.random.fold_in(key, 3), *heavy), -limit, limit).astype(kind)


def setup_inputs(seed: int = 0) -> dict:
    key_list = jax.random.split(jax.random.key(seed), 6)
    features = bell_draw_with(key_list[0], (MEMBERS, D, CELLS), 1.0, 6.0, ((0, 8), (2, 16)), (2, 1, 16, 2.0))
    up_weight = noise(key_list[1], (D, D), D ** -0.5, 0.1875)
    out_weight = noise(key_list[2], (D, C), D ** -0.5, 0.1875)
    target = noise(key_list[3], (C, CELLS), 1.0, 6.0, ((1, 16),))
    area = jnp.clip(jnp.exp(math.log(1.0) - 2.3025851 * jax.random.uniform(key_list[4], (CELLS,), jnp.float32) ** shard_levels(key_list[4], (CELLS,), ((0, 16),), -0.2, 0.2)), 0.1, 1.0)
    return dict(features=features, up_weight=up_weight, out_weight=out_weight, target=target, area=area)


def smooth(diff):
    return diff * lax.rsqrt(diff * diff + 0.0625)

def silu_slope(pre):
    sig = jax.nn.sigmoid(pre)
    return sig * (1.0 + pre * (1.0 - sig))

def forward(xm, up_weight, out_weight):
    pre = jnp.dot(up_weight.T, xm, preferred_element_type=jnp.float32)
    hidden = jax.nn.silu(pre).astype(jnp.bfloat16)
    pred = jnp.dot(out_weight.T, hidden, preferred_element_type=jnp.float32)
    return pred

def reference(features, up_weight, out_weight, target, area):
    preds = lax.map(lambda xm: forward(xm, up_weight, out_weight), features)
    members = preds.shape[0]

    def pair_of(pm):
        return lax.optimization_barrier(jnp.sum(smooth(pm[None] - preds), axis=0))
    pairs = lax.map(pair_of, preds)
    tgt = target.astype(jnp.float32)

    def backward(carry, inputs):
        xm, pm, pair = inputs
        pre = jnp.dot(up_weight.T, xm, preferred_element_type=jnp.float32)
        hidden = jax.nn.silu(pre).astype(jnp.bfloat16)
        pgrad = (area[None, :] * (smooth(pm - tgt) / members - 0.95 / (members * (members - 1)) * pair)).astype(jnp.bfloat16)
        hgrad = jnp.dot(out_weight, pgrad, preferred_element_type=jnp.float32)
        pre_grad = (hgrad * silu_slope(pre)).astype(jnp.bfloat16)
        xgrad = jnp.dot(up_weight, pre_grad, preferred_element_type=jnp.float32).astype(jnp.bfloat16)
        ug = carry[0] + jnp.dot(xm, pre_grad.T, preferred_element_type=jnp.float32)
        og = carry[1] + jnp.dot(hidden, pgrad.T, preferred_element_type=jnp.float32)
        return ((ug, og), xgrad)
    start = (jnp.zeros((D, D), jnp.float32), jnp.zeros((D, C), jnp.float32))
    (ug, og), xgrads = lax.scan(backward, start, (features, preds, pairs))
    scale = 1.0 / math.sqrt(CELLS * MEMBERS)
    return (xgrads, ug * scale, og * scale)
```

```python
import functools
import math

import jax
import jax.numpy as jnp
from jax import lax
from jax.experimental import pallas as pl
from jax.experimental.pallas import tpu as pltpu
from jax.sharding import Mesh
from jax.sharding import PartitionSpec as P


MEMBER = ("z", "ylo")
CHIP = ("z", "ylo", "x", "yhi")
SPACE = ("x", "yhi", "core")
DEVICE = ("z", "ylo", "x", "yhi", "core")

FIRST = ((2, 1), (2, 0), (1, 1), (3, 1))
SECOND = ((1, 0), (3, 0), (0, 1), (0, 0))
EARLY = ((0, 0), (0, 1), (1, 0), (3, 0))
LATE = ((1, 1), (3, 1), (2, 0), (2, 1))

TILE = 512
STRIP = 256
SPAN = 1024
ROWS = 256
MIB = 1 << 20
BF16, F32 = jnp.bfloat16, jnp.float32


def route(slot, back):
    pairs = []
    for z in range(4):
        for y in range(2):
            here, there = 2 * z + y, 2 * ((z + slot[0]) % 4) + (y ^ slot[1])
            pairs.append((there, here) if back else (here, there))
    return pairs


def in_hbm(x):
    return pltpu.with_memory_space_constraint(x, pltpu.HBM)


def in_vmem(x):
    return pltpu.with_memory_space_constraint(x, pltpu.VMEM)


def smooth(diff):
    return diff * lax.rsqrt(diff * diff + 0.0625)


def mm(a, b, ca, cb):
    return lax.dot_general(a, b, (((ca,), (cb,)), ((), ())), preferred_element_type=F32)


def forward_kernel(first, tiles, *refs):
    if first:
        x, w, owt, hidden, slope, *preds, wt = refs
    else:
        x, wt, owt, _, _, hidden, slope, *preds = refs
    step = pl.program_id(0)

    if first:

        @pl.when(step == 0)
        def _():
            for i in range(0, w.shape[0], ROWS):
                wt[:, i : i + ROWS] = w[i : i + ROWS, :].T

    xt = x[...]
    for j in range(0, wt.shape[0], ROWS):
        rows = slice(j, j + ROWS)
        pre = mm(wt[rows, :], xt, 1, 0)
        twice = jnp.tanh(0.5 * pre) + 1.0
        sig = 0.5 * twice
        act = pre * sig
        hidden[rows, :] = act.astype(BF16)
        slope[rows, :] = (sig + act * (1.0 - sig)).astype(BF16)
    pred = mm(owt[...], hidden[...], 1, 0)
    pieces = TILE // STRIP
    for i, out in enumerate(preds):
        for k in range(pieces):

            @pl.when(step == i * pieces + k)
            def _():
                out[:, k * STRIP : (k + 1) * STRIP] = pred


def forward(tiles, x, w, owt, carried=None):
    first = carried is None
    depth, cells = x.shape
    channels = owt.shape[0]
    n = tiles.shape[0]
    pieces = TILE // STRIP
    at_tile = pl.BlockSpec((depth, STRIP), lambda g, t: (0, t[g // pieces] * pieces + g % pieces))
    fixed = pl.BlockSpec(memory_space=pltpu.VMEM)
    any_spec = pl.BlockSpec(memory_space=pl.ANY)
    act = pltpu.HBM((depth, cells), BF16)
    out_shape = [act, act] + [pltpu.VMEM((channels, TILE), F32)] * n
    out_specs = [at_tile, at_tile] + [fixed] * n
    if not first:
        out_shape[-1] = pltpu.HBM((channels, TILE), F32)
        out_specs[-1] = pl.BlockSpec((channels, TILE), lambda g, t: (0, 0))
    args, in_specs, alias = [in_hbm(x), in_vmem(w), in_vmem(owt)], [at_tile, fixed, fixed], {}
    if first:
        out_shape.append(pltpu.VMEM((depth, depth), BF16))
        out_specs.append(fixed)
    else:
        args += list(carried)
        in_specs += [any_spec, any_spec]
        alias = {4: 0, 5: 1}
    return pl.pallas_call(
        functools.partial(forward_kernel, first),
        grid_spec=pltpu.PrefetchScalarGridSpec(
            num_scalar_prefetch=1, grid=(n * pieces,), in_specs=in_specs, out_specs=out_specs
        ),
        out_shape=out_shape,
        input_output_aliases=alias,
        compiler_params=pltpu.CompilerParams(vmem_limit_bytes=32 * MIB),
        cost_estimate=pl.CostEstimate(
            flops=2 * depth * (depth + channels) * TILE * n,
            bytes_accessed=6 * depth * TILE * n + 2 * depth * depth,
            transcendentals=depth * TILE * n,
        ),
        name="forward",
    )(tiles, *args)


def pair_kernel(members, me, *refs):
    preds, target, area, outs = refs[:members], refs[members], refs[members + 1], refs[members + 2 :]
    across = 0.95 / (members * (members - 1))
    channels = preds[0].shape[0]
    for lane in range(0, TILE, 128):
        cols = slice(lane, lane + 128)
        weight = area[:, cols]
        for low in range(0, channels, 8):
            rows = slice(low, min(low + 8, channels))
            p = [r[rows, cols] for r in preds]
            t = target[rows, cols].astype(F32)
            total = [None] * members
            for a in range(members):
                for b in range(a + 1, members):
                    s = smooth(p[a] - p[b])
                    total[a] = s if total[a] is None else total[a] + s
                    total[b] = -s if total[b] is None else total[b] - s
            for a in range(members):
                g = weight * (smooth(p[a] - t) * (1.0 / members) - across * total[a])
                outs[a][rows, cols] = g.astype(BF16).astype(F32)


def pairs(me, preds, target, area):
    members = len(preds)
    channels = preds[0].shape[0]
    fixed = pl.BlockSpec(memory_space=pltpu.VMEM)
    return pl.pallas_call(
        functools.partial(pair_kernel, members),
        grid_spec=pltpu.PrefetchScalarGridSpec(
            num_scalar_prefetch=1,
            grid=(1,),
            in_specs=[fixed] * (members - 1)
            + [
                pl.BlockSpec((channels, TILE), lambda g, t: (0, 0)),
                pl.BlockSpec((channels, TILE), lambda g, t: (0, t[0])),
                pl.BlockSpec((1, TILE), lambda g, t: (0, t[0])),
            ],
            out_specs=[fixed] * (members - 1)
            + [pl.BlockSpec((channels, TILE), lambda g, t: (0, 0))],
        ),
        out_shape=[pltpu.VMEM((channels, TILE), F32)] * (members - 1)
        + [pltpu.HBM((channels, TILE), F32)],
        compiler_params=pltpu.CompilerParams(vmem_limit_bytes=16 * MIB),
        cost_estimate=pl.CostEstimate(
            flops=36 * 6 * channels * TILE,
            bytes_accessed=8 * members * channels * TILE,
            transcendentals=36 * channels * TILE,
        ),
        name="pairs",
    )(me, *map(in_vmem, preds[:-1]), in_hbm(preds[-1]), target, area)


def backward_kernel(chunks, table, *refs):
    n = table.shape[0] - 1
    grads = refs[:n]
    x_hbm, hidden, slope, owt, grad, away, keep, pg, acc, out, x, sem = refs[n:]
    block, chunk = pl.program_id(0), pl.program_id(1)
    channels, wide = pg.shape[0], grad.shape[1]

    def fetch(c):
        cols = pl.ds(pl.multiple_of(c * wide, wide), wide)
        return pltpu.make_async_copy(x_hbm.at[:, cols], x.at[:, cols], sem.at[c])

    @pl.when((block == 0) & (chunk == 0))
    def _():
        for c in range(chunks):
            fetch(c).start()
        for i, ref in enumerate(grads):
            pg[:, pl.ds(pl.multiple_of(table[i] * TILE, TILE), TILE)] = ref[...].astype(BF16)

    @pl.when(chunk == 0)
    def _():
        acc[...] = jnp.zeros_like(acc)
        out[...] = jnp.zeros_like(out)

    @pl.when(block == 0)
    def _():
        fetch(chunk).wait()

    span = pl.ds(pl.multiple_of(chunk * wide, wide), wide)
    pgt = pg[:, span]
    for low in range(0, wide, ROWS):
        cols = slice(low, low + ROWS)
        hg = mm(owt[...], pgt[:, cols], 0, 0)
        grad[:, cols] = (hg * slope[:, cols].astype(F32)).astype(BF16)
    out[:channels, :] += mm(pgt, hidden[...], 1, 1)
    acc[...] += mm(x[:, span], grad[...], 1, 1)

    @pl.when(chunk == chunks - 1)
    def _():
        mine = table[n] * 8
        own = pl.ds(pl.multiple_of(block * ROWS, ROWS), ROWS)
        depth = acc.shape[0]
        for c in range(keep.shape[0]):
            for ref, low in ((keep, c * 16 + mine), (away, c * 16 + 8 - mine)):
                ref[c, :, own] = acc[pl.ds(pl.multiple_of(low, 8), 8), :]
        acc[:ROWS, :128] = out[...].T
        each = ROWS // 16
        for c in range(each):
            for ref, low in ((keep, c * 16 + mine), (away, c * 16 + 8 - mine)):
                rows = acc[pl.ds(pl.multiple_of(low, 8), 8), :128]
                ref[block * each + c, :, depth:] = rows


def backward(table, grads, x, hidden, slope, owt):
    depth, cells = x.shape
    channels = owt.shape[0]
    chips, wide = depth // 16, depth + 128
    blocks, chunks = depth // ROWS, cells // SPAN
    at = pl.BlockSpec((ROWS, SPAN), lambda b, c, t: (b, c))
    fixed = pl.BlockSpec(memory_space=pltpu.VMEM)
    return pl.pallas_call(
        functools.partial(backward_kernel, chunks),
        grid_spec=pltpu.PrefetchScalarGridSpec(
            num_scalar_prefetch=1,
            grid=(blocks, chunks),
            in_specs=[pl.BlockSpec((channels, TILE), lambda b, c, t: (0, 0))]
            + [fixed] * (len(grads) - 1)
            + [
                pl.BlockSpec(memory_space=pl.ANY),
                at,
                at,
                pl.BlockSpec((channels, ROWS), lambda b, c, t: (0, b)),
            ],
            out_specs=[at, fixed, fixed],
            scratch_shapes=[
                pltpu.VMEM((channels, cells), BF16),
                pltpu.VMEM((depth, ROWS), F32),
                pltpu.VMEM((128, ROWS), F32),
                pltpu.VMEM((depth, cells), BF16),
                pltpu.SemaphoreType.DMA((chunks,)),
            ],
        ),
        out_shape=[pltpu.HBM((depth, cells), BF16)] + [pltpu.VMEM((chips, 8, wide), F32)] * 2,
        compiler_params=pltpu.CompilerParams(vmem_limit_bytes=36 * MIB),
        cost_estimate=pl.CostEstimate(
            flops=2 * depth * (depth + 2 * channels) * cells,
            bytes_accessed=8 * depth * cells + 4 * depth * depth,
            transcendentals=0,
        ),
        name="backward",
    )(table, in_hbm(grads[0]), *map(in_vmem, grads[1:]), in_hbm(x), in_hbm(hidden), in_hbm(slope), owt)


def feature_kernel(w, grad, out):
    g = grad[...]
    for i in range(0, w.shape[0], ROWS):
        rows = slice(i, i + ROWS)
        out[0, rows, :] = mm(w[rows, :], g, 1, 0).astype(BF16)


def feature_grad(w, grad):
    depth, cells = grad.shape
    return pl.pallas_call(
        feature_kernel,
        grid=(cells // TILE,),
        in_specs=[
            pl.BlockSpec(memory_space=pltpu.VMEM),
            pl.BlockSpec((depth, TILE), lambda g: (0, g)),
        ],
        out_specs=pl.BlockSpec((1, depth, TILE), lambda g: (0, 0, g)),
        out_shape=jax.ShapeDtypeStruct((1, depth, cells), BF16),
        compiler_params=pltpu.CompilerParams(vmem_limit_bytes=24 * MIB),
        cost_estimate=pl.CostEstimate(
            flops=2 * depth * depth * cells,
            bytes_accessed=4 * depth * cells + 2 * depth * depth,
            transcendentals=0,
        ),
        name="feature_grad",
    )(w, in_hbm(grad))


def total_kernel(scale, parts, up, out):
    depth, channels = up.shape[1], out.shape[1]
    acc = parts[0]
    for c in range(1, parts.shape[0]):
        acc = acc + parts[c]
    acc = acc * scale
    up[...] = acc[:, :depth]
    out[...] = acc[:, depth : depth + channels]


def total(parts, depth, channels, scale):
    rows = parts.shape[1]
    return pl.pallas_call(
        functools.partial(total_kernel, scale),
        in_specs=[pl.BlockSpec(memory_space=pltpu.VMEM)],
        out_shape=[
            jax.ShapeDtypeStruct((rows, depth), F32),
            jax.ShapeDtypeStruct((rows, channels), F32),
        ],
        compiler_params=pltpu.CompilerParams(vmem_limit_bytes=16 * MIB),
        name="total",
    )(parts)


def spread(away, keep):
    swapped = lax.ppermute(away, "core", [(0, 1), (1, 0)])
    return lax.all_to_all(keep + swapped, CHIP, 0, 0, tiled=True)


def body(features, up_weight, out_weight, target, area):
    x = features[0]
    depth, cells = x.shape
    channels = out_weight.shape[1]
    owt = out_weight.T
    z, y = lax.axis_index("z"), lax.axis_index("ylo")
    me = jnp.reshape(2 * z + y, (1,)).astype(jnp.int32)
    core = lax.axis_index("core")

    def tile_of(slot):
        return 2 * lax.rem(z + slot[0], 4) + lax.bitwise_xor(y, slot[1])

    def table(slots, *more):
        return jnp.stack([tile_of(s) for s in slots] + list(more)).astype(jnp.int32)

    one = forward(table(FIRST), x, up_weight, owt)
    wt = one[-1]
    pred = dict(zip(FIRST, one[2:-1]))
    two = forward(table(SECOND), x, wt, owt, (one[0], one[1]))
    hidden, slope = two[:2]
    pred.update(zip(SECOND, two[2:]))

    order = FIRST + SECOND
    got = [pred[s] if s == (0, 0) else lax.ppermute(pred[s], MEMBER, route(s, False)) for s in order]
    given = dict(zip(order, pairs(me, got, target, area[None, :])))
    grad = {
        s: given[s] if s == (0, 0) else lax.ppermute(given[s], MEMBER, route(s, True))
        for s in EARLY + LATE
    }

    order = EARLY + LATE
    pre_grad, away, keep = backward(
        table(order, core), [grad[s] for s in order], x, hidden, slope, owt
    )
    parts = spread(away, keep)
    fgrad = feature_grad(up_weight, pre_grad)
    scale = 1.0 / math.sqrt(cells * lax.axis_size(SPACE) * lax.axis_size(MEMBER))
    up_grad, out_grad = total(parts, depth, channels, scale)
    return fgrad, up_grad, out_grad


def solution(mesh):
    fine = Mesh(mesh.devices.reshape(4, 2, 4, 2, 2), DEVICE)
    in_specs = (P(MEMBER, None, SPACE), P(), P(), P(None, SPACE), P(SPACE))
    out_specs = (P(MEMBER, None, SPACE), P(DEVICE, None), P(DEVICE, None))
    return jax.shard_map(body, mesh=fine, in_specs=in_specs, out_specs=out_specs, check_vma=False)
```

```python
import functools
import math

import jax
import jax.numpy as jnp
from jax import lax
from jax.experimental import pallas as pl
from jax.experimental.pallas import tpu as pltpu
from jax.sharding import Mesh
from jax.sharding import PartitionSpec as P


MEMBER = ("z", "ylo")
CHIP = ("z", "ylo", "x", "yhi")
SPACE = ("x", "yhi", "core")
DEVICE = ("z", "ylo", "x", "yhi", "core")

SLOTS = ((0, 0), (0, 1), (1, 0), (3, 0), (1, 1), (3, 1), (2, 0), (2, 1))
FIRST = ((2, 1), (2, 0), (1, 1), (3, 1), (0, 1))
SECOND = ((1, 0), (3, 0), (0, 0))
PARTS = 2

TILE = 512
ROWS = 256
MIB = 1 << 20
BF16, F32 = jnp.bfloat16, jnp.float32


def route(slot, back):
    pairs = []
    for z in range(4):
        for y in range(2):
            here, there = 2 * z + y, 2 * ((z + slot[0]) % 4) + (y ^ slot[1])
            pairs.append((there, here) if back else (here, there))
    return pairs


def in_hbm(x):
    return pltpu.with_memory_space_constraint(x, pltpu.HBM)


def in_vmem(x):
    return pltpu.with_memory_space_constraint(x, pltpu.VMEM)


def smooth(diff):
    return diff * lax.rsqrt(diff * diff + 0.0625)


def mm(a, b, ca, cb):
    return lax.dot_general(a, b, (((ca,), (cb,)), ((), ())), preferred_element_type=F32)


def forward_kernel(first, tiles, *refs):
    if first:
        x, w, owt, hidden, slope, *preds, wt, ow = refs
    else:
        x, wt, owt, _, _, hidden, slope, *preds = refs
    step = pl.program_id(0)

    if first:

        @pl.when(step == 0)
        def _():
            for i in range(0, w.shape[0], ROWS):
                wt[:, i : i + ROWS] = (w[i : i + ROWS, :] * 0.5).T
            ow[...] = (owt[...] * 0.5).T

    h = mm(wt[...], x[...], 1, 0)
    u = jnp.tanh(h) + 1.0
    act = h * u
    hidden[...] = act.astype(BF16)
    slope[...] = (u + act * (2.0 - u)).astype(BF16)
    pred = mm(owt[...], hidden[...], 1, 0)
    for i, out in enumerate(preds):

        @pl.when(step == i)
        def _():
            out[...] = pred


def forward(table, x, w, owt, carried=None):
    first = carried is None
    depth, cells = x.shape
    channels = owt.shape[0]
    n = table.shape[0] // 2
    at_tile = pl.BlockSpec((depth, TILE), lambda g, t: (0, t[g]))
    at_slot = pl.BlockSpec((depth, TILE), lambda g, t: (0, t[n + g]))
    whole = lambda *s: pl.BlockSpec(s, lambda g, t: (0,) * len(s))
    fixed = pl.BlockSpec(memory_space=pltpu.VMEM)
    any_spec = pl.BlockSpec(memory_space=pl.ANY)
    act = pltpu.HBM((depth, cells), BF16)
    out_shape = [act, act] + [pltpu.VMEM((channels, TILE), F32)] * n
    out_specs = [at_slot, at_slot] + [fixed] * n
    if not first:
        out_shape[-1] = pltpu.HBM((channels, TILE), F32)
        out_specs[-1] = pl.BlockSpec((channels, TILE), lambda g, t: (0, 0))
    w_spec = whole(depth, depth) if first else fixed
    w = in_hbm(w) if first else in_vmem(w)
    args, in_specs = [in_hbm(x), w, in_hbm(owt)], [at_tile, w_spec, whole(channels, depth)]
    alias = {}
    if first:
        out_shape += [pltpu.VMEM((depth, depth), BF16), pltpu.VMEM((depth, channels), BF16)]
        out_specs += [fixed, fixed]
    else:
        args += list(carried)
        in_specs += [any_spec, any_spec]
        alias = {4: 0, 5: 1}
    return pl.pallas_call(
        functools.partial(forward_kernel, first),
        grid_spec=pltpu.PrefetchScalarGridSpec(
            num_scalar_prefetch=1, grid=(n,), in_specs=in_specs, out_specs=out_specs
        ),
        out_shape=out_shape,
        input_output_aliases=alias,
        compiler_params=pltpu.CompilerParams(vmem_limit_bytes=32 * MIB),
        cost_estimate=pl.CostEstimate(
            flops=2 * depth * (depth + channels) * TILE * n,
            bytes_accessed=6 * depth * TILE * n + 2 * depth * depth,
            transcendentals=depth * TILE * n,
        ),
        name="forward",
    )(table, *args)


def pair_kernel(members, table, *refs):
    preds, target, area, outs = refs[:members], refs[members], refs[members + 1], refs[members + 2 :]
    across = 0.95 / (members * (members - 1))
    channels = preds[0].shape[0]
    for lane in range(0, TILE, 128):
        cols = slice(lane, lane + 128)
        weight = area[:, cols]
        for low in range(0, channels, 8):
            rows = slice(low, min(low + 8, channels))
            p = [r[rows, cols] for r in preds]
            t = target[rows, cols].astype(F32)
            total = [None] * members
            for a in range(members):
                for b in range(a + 1, members):
                    s = smooth(p[a] - p[b])
                    total[a] = s if total[a] is None else total[a] + s
                    total[b] = -s if total[b] is None else total[b] - s
            for a in range(members):
                g = weight * (smooth(p[a] - t) * (1.0 / members) - across * total[a])
                outs[a][rows, cols] = g.astype(BF16).astype(F32)


def pairs(table, preds, target, area):
    members = len(preds)
    channels = preds[0].shape[0]
    fixed = pl.BlockSpec(memory_space=pltpu.VMEM)
    return pl.pallas_call(
        functools.partial(pair_kernel, members),
        grid_spec=pltpu.PrefetchScalarGridSpec(
            num_scalar_prefetch=1,
            grid=(1,),
            in_specs=[fixed] * (members - 1)
            + [
                pl.BlockSpec((channels, TILE), lambda g, t: (0, 0)),
                pl.BlockSpec((channels, TILE), lambda g, t: (0, t[0])),
                pl.BlockSpec((1, TILE), lambda g, t: (0, t[0])),
            ],
            out_specs=[fixed] * (members - 1)
            + [pl.BlockSpec((channels, TILE), lambda g, t: (0, 0))],
        ),
        out_shape=[pltpu.VMEM((channels, TILE), F32)] * (members - 1)
        + [pltpu.HBM((channels, TILE), F32)],
        compiler_params=pltpu.CompilerParams(vmem_limit_bytes=16 * MIB),
        cost_estimate=pl.CostEstimate(
            flops=36 * 6 * channels * TILE,
            bytes_accessed=8 * members * channels * TILE,
            transcendentals=36 * channels * TILE,
        ),
        name="pairs",
    )(table, *map(in_vmem, preds[:-1]), in_hbm(preds[-1]), target, area)


def backward_kernel(part, n, info, *refs):
    grads, refs = refs[:n], refs[n:]
    last = part == PARTS - 1
    if last:
        x, hidden, slope, ow, up_in, out_in, _, grad, away, keep, pg, up, out = refs
    else:
        x_hbm, hidden, slope, ow, grad, up, out, held, pg, x, sem = refs
    block = pl.program_id(0)
    channels, wide = pg.shape

    def fetch(i):
        tile = pl.ds(pl.multiple_of(info[1 + i] * TILE, TILE), TILE)
        place = slice(i % n * TILE, (i % n + 1) * TILE)
        return pltpu.make_async_copy(x_hbm.at[:, tile], (x, held)[i // n].at[:, place], sem.at[i])

    if not last:

        @pl.when(block == 0)
        def _():
            for i in range(2 * n):
                fetch(i).start()

    @pl.when(block == 0)
    def _():
        for i, ref in enumerate(grads):
            pg[:, i * TILE : (i + 1) * TILE] = ref[...].astype(BF16)

    for low in range(0, wide, ROWS):
        cols = slice(low, low + ROWS)
        hg = mm(ow[...], pg[:, cols], 1, 0)
        grad[:, cols] = (hg * slope[:, cols].astype(F32)).astype(BF16)
    part_out = mm(pg[...], hidden[...], 1, 1)
    if not last:

        @pl.when(block == 0)
        def _():
            for i in range(n):
                fetch(i).wait()

    part_up = mm(x[...], grad[...], 1, 1)
    shape = up.shape[-4:]
    if not last:
        up[block] = part_up.reshape(shape)
        out[block, :channels, :] = part_out

        @pl.when(block == pl.num_programs(0) - 1)
        def _():
            for i in range(n, 2 * n):
                fetch(i).wait()

    else:
        chips, depth = keep.shape[0], keep.shape[2] - 128
        own = pl.ds(pl.multiple_of(block * ROWS, ROWS), ROWS)
        each = ROWS // 16
        rows = pl.ds(block * each, each)
        up[...] = part_up.reshape(shape) + up_in[block]
        turned = (part_out + out_in[block, :channels, :]).T
        out[..., :channels] = turned.reshape(each, 2, 8, channels)
        for ref, side in ((keep, info[0]), (away, 1 - info[0])):
            ref[:, :, own] = up[:, side]
            ref[rows, :, depth:] = out[:, side]


def backward(part, info, grads, x, hidden, slope, ow, carried=None):
    last = part == PARTS - 1
    depth, cells = hidden.shape
    channels = ow.shape[1]
    chips, blocks, wide = depth // 16, depth // ROWS, cells // PARTS
    at = pl.BlockSpec((ROWS, wide), lambda b, t: (b, part))
    fixed = pl.BlockSpec(memory_space=pltpu.VMEM)
    one = pl.BlockSpec((channels, TILE), lambda b, t: (0, 0))
    in_specs = [one if part == 0 and i == 0 else fixed for i in range(len(grads))]
    in_specs += [fixed if last else pl.BlockSpec(memory_space=pl.ANY)]
    in_specs += [at, at, pl.BlockSpec((ROWS, channels), lambda b, t: (b, 0))]
    args = [in_hbm(g) if s is one else in_vmem(g) for g, s in zip(grads, in_specs)]
    args += [in_vmem(x) if last else in_hbm(x), in_hbm(hidden), in_hbm(slope), ow]
    out_shape, out_specs = [pltpu.HBM((depth, cells), BF16)], [at]
    scratch = [pltpu.VMEM((channels, wide), BF16)]
    alias = {}
    if last:
        args += [in_vmem(carried[1]), in_vmem(carried[2]), carried[0]]
        in_specs += [fixed, fixed, pl.BlockSpec(memory_space=pl.ANY)]
        alias = {len(args): 0}
        out_shape += [pltpu.VMEM((chips, 8, depth + 128), F32)] * 2
        scratch += [pltpu.VMEM((chips, 2, 8, ROWS), F32), pltpu.VMEM((ROWS // 16, 2, 8, 128), F32)]
    else:
        out_shape += [
            pltpu.VMEM((blocks, chips, 2, 8, ROWS), F32),
            pltpu.VMEM((blocks, 128, ROWS), F32),
            pltpu.VMEM((depth, wide), BF16),
        ]
        scratch += [pltpu.VMEM((depth, wide), BF16), pltpu.SemaphoreType.DMA((2 * len(grads),))]
    out_specs += [fixed] * (len(out_shape) - 1)
    return pl.pallas_call(
        functools.partial(backward_kernel, part, len(grads)),
        grid_spec=pltpu.PrefetchScalarGridSpec(
            num_scalar_prefetch=1,
            grid=(blocks,),
            in_specs=in_specs,
            out_specs=out_specs,
            scratch_shapes=scratch,
        ),
        out_shape=out_shape,
        input_output_aliases=alias,
        compiler_params=pltpu.CompilerParams(vmem_limit_bytes=24 * MIB),
        cost_estimate=pl.CostEstimate(
            flops=2 * depth * (depth + 2 * channels) * wide,
            bytes_accessed=6 * depth * wide,
            transcendentals=0,
        ),
        name="backward",
    )(info, *args)


def feature_kernel(table, w, grad, out):
    out[0] = mm(w[...], grad[...], 1, 0).astype(BF16)


def feature_grad(table, w, grad):
    depth, cells = grad.shape
    return pl.pallas_call(
        feature_kernel,
        grid_spec=pltpu.PrefetchScalarGridSpec(
            num_scalar_prefetch=1,
            grid=(cells // TILE,),
            in_specs=[
                pl.BlockSpec((depth, depth), lambda g, t: (0, 0)),
                pl.BlockSpec((depth, TILE), lambda g, t: (0, g)),
            ],
            out_specs=pl.BlockSpec((1, depth, TILE), lambda g, t: (0, 0, t[g])),
        ),
        out_shape=jax.ShapeDtypeStruct((1, depth, cells), BF16),
        compiler_params=pltpu.CompilerParams(vmem_limit_bytes=24 * MIB),
        cost_estimate=pl.CostEstimate(
            flops=2 * depth * depth * cells,
            bytes_accessed=4 * depth * cells + 2 * depth * depth,
            transcendentals=0,
        ),
        name="feature_grad",
    )(table, in_hbm(w), in_hbm(grad))


def total_kernel(scale, parts, up, out):
    depth, channels = up.shape[1], out.shape[1]
    acc = parts[0]
    for c in range(1, parts.shape[0]):
        acc = acc + parts[c]
    acc = acc * scale
    up[...] = acc[:, :depth]
    out[...] = acc[:, depth : depth + channels]


def total(parts, depth, channels, scale):
    rows = parts.shape[1]
    return pl.pallas_call(
        functools.partial(total_kernel, scale),
        in_specs=[pl.BlockSpec(memory_space=pltpu.VMEM)],
        out_shape=[
            jax.ShapeDtypeStruct((rows, depth), F32),
            jax.ShapeDtypeStruct((rows, channels), F32),
        ],
        compiler_params=pltpu.CompilerParams(vmem_limit_bytes=16 * MIB),
        name="total",
    )(parts)


def spread(away, keep):
    swapped = lax.ppermute(away, "core", [(0, 1), (1, 0)])
    return lax.all_to_all(keep + swapped, CHIP, 0, 0, tiled=True)


def body(features, up_weight, out_weight, target, area):
    x = features[0]
    depth, cells = x.shape
    channels = out_weight.shape[1]
    owt = out_weight.T
    z, y = lax.axis_index("z"), lax.axis_index("ylo")
    core = lax.axis_index("core")

    def tile_of(slot):
        return 2 * lax.rem(z + slot[0], 4) + lax.bitwise_xor(y, slot[1])

    def table(slots):
        return jnp.stack([tile_of(s) for s in slots]).astype(jnp.int32)

    def plan(slots):
        return jnp.stack(
            [tile_of(s) for s in slots] + [jnp.int32(SLOTS.index(s)) for s in slots]
        ).astype(jnp.int32)

    one = forward(plan(FIRST), x, up_weight, owt)
    wt, ow = one[-2:]
    pred = dict(zip(FIRST, one[2:-2]))
    two = forward(plan(SECOND), x, wt, owt, (one[0], one[1]))
    hidden, slope = two[:2]
    pred.update(zip(SECOND, two[2:]))

    order = FIRST + SECOND
    tiles = table(SLOTS)
    got = [pred[s] if s == (0, 0) else lax.ppermute(pred[s], MEMBER, route(s, False)) for s in order]
    given = dict(zip(order, pairs(tiles, got, target, area[None, :])))
    grad = [
        given[s] if s == (0, 0) else lax.ppermute(given[s], MEMBER, route(s, True)) for s in SLOTS
    ]

    half = len(SLOTS) // PARTS
    info = jnp.concatenate([jnp.reshape(core, (1,)).astype(jnp.int32), tiles])
    *some, held = backward(0, info, grad[:half], x, hidden, slope, ow)
    pre_grad, away, keep = backward(1, info, grad[half:], held, hidden, slope, ow, some)
    parts = spread(away, keep)
    fgrad = feature_grad(tiles, up_weight, pre_grad)
    scale = 1.0 / math.sqrt(cells * lax.axis_size(SPACE) * lax.axis_size(MEMBER))
    up_grad, out_grad = total(parts, depth, channels, scale)
    return fgrad, up_grad, out_grad


def solution(mesh):
    fine = Mesh(mesh.devices.reshape(4, 2, 4, 2, 2), DEVICE)
    in_specs = (P(MEMBER, None, SPACE), P(), P(), P(None, SPACE), P(SPACE))
    out_specs = (P(MEMBER, None, SPACE), P(DEVICE, None), P(DEVICE, None))
    return jax.shard_map(body, mesh=fine, in_specs=in_specs, out_specs=out_specs, check_vma=False)
```

```python
import functools
import math

import jax
import jax.numpy as jnp
from jax import lax
from jax.experimental import pallas as pl
from jax.experimental.pallas import tpu as pltpu
from jax.sharding import Mesh
from jax.sharding import PartitionSpec as P


MEMBER = ("z", "ylo")
CHIP = ("z", "ylo", "x", "yhi")
SPACE = ("x", "yhi", "core")
DEVICE = ("z", "ylo", "x", "yhi", "core")

NEAR = ((1, 0), (3, 0), (1, 1), (3, 1))
SIDE = ((0, 0), (0, 1))
FAR = ((2, 0), (2, 1))
SLOTS = NEAR + SIDE + FAR

TILE = 512
HALF = 256
ROWS = 256
MIB = 1 << 20
BF16, F32 = jnp.bfloat16, jnp.float32


def route(slot, back):
    pairs = []
    for z in range(4):
        for y in range(2):
            here, there = 2 * z + y, 2 * ((z + slot[0]) % 4) + (y ^ slot[1])
            pairs.append((there, here) if back else (here, there))
    return pairs


def in_hbm(x):
    return pltpu.with_memory_space_constraint(x, pltpu.HBM)


def in_vmem(x):
    return pltpu.with_memory_space_constraint(x, pltpu.VMEM)


def smooth(diff):
    return diff * lax.rsqrt(diff * diff + 0.0625)


def mm(a, b, ca, cb):
    return lax.dot_general(a, b, (((ca,), (cb,)), ((), ())), preferred_element_type=F32)


def forward_kernel(first, tiles, *refs):
    if first:
        x, w, owt, hidden, slope, *preds, wt, ow = refs
    else:
        x, wt, owt, _, _, hidden, slope, *preds = refs
    step = pl.program_id(0)

    if first:

        @pl.when(step == 0)
        def _():
            for i in range(0, w.shape[0], ROWS):
                wt[:, i : i + ROWS] = (w[i : i + ROWS, :] * 0.5).T
            ow[...] = (owt[...] * 0.5).T

    h = mm(wt[...], x[...], 1, 0)
    u = jnp.tanh(h) + 1.0
    act = h * u
    hidden[...] = act.astype(BF16)
    slope[...] = (u + act * (2.0 - u)).astype(BF16)
    pred = mm(owt[...], hidden[...], 1, 0)
    if not first:
        for i, out in enumerate(preds):

            @pl.when(step == i)
            def _():
                out[...] = pred

        return
    for i, out in enumerate(preds):

        @pl.when(step == i)
        def _():
            out[:, :TILE] = pred

    for i in range(2):

        @pl.when(step == len(preds) + i)
        def _():
            preds[2 * i][:, TILE:] = pred[:, :HALF]
            preds[2 * i + 1][:, TILE:] = pred[:, HALF:]


def forward(table, x, w, owt, carried=None):
    first = carried is None
    depth, cells = x.shape
    channels = owt.shape[0]
    n = table.shape[0] // 2
    at_tile = pl.BlockSpec((depth, TILE), lambda g, t: (0, t[g]))
    at_slot = pl.BlockSpec((depth, TILE), lambda g, t: (0, t[n + g]))
    whole = lambda *s: pl.BlockSpec(s, lambda g, t: (0,) * len(s))
    fixed = pl.BlockSpec(memory_space=pltpu.VMEM)
    any_spec = pl.BlockSpec(memory_space=pl.ANY)
    act = pltpu.HBM((depth, cells), BF16)
    if first:
        out_shape = [act, act] + [pltpu.VMEM((channels, TILE + HALF), F32)] * 4
        out_specs = [at_slot, at_slot] + [fixed] * 4
    else:
        out_shape = [act, act, pltpu.HBM((channels, TILE), F32), pltpu.VMEM((channels, TILE), F32)]
        out_specs = [at_slot, at_slot, whole(channels, TILE), fixed]
    w_spec = whole(depth, depth) if first else fixed
    w = in_hbm(w) if first else in_vmem(w)
    args, in_specs = [in_hbm(x), w, in_hbm(owt)], [at_tile, w_spec, whole(channels, depth)]
    alias = {}
    if first:
        out_shape += [pltpu.VMEM((depth, depth), BF16), pltpu.VMEM((depth, channels), BF16)]
        out_specs += [fixed, fixed]
    else:
        args += list(carried)
        in_specs += [any_spec, any_spec]
        alias = {4: 0, 5: 1}
    return pl.pallas_call(
        functools.partial(forward_kernel, first),
        grid_spec=pltpu.PrefetchScalarGridSpec(
            num_scalar_prefetch=1, grid=(n,), in_specs=in_specs, out_specs=out_specs
        ),
        out_shape=out_shape,
        input_output_aliases=alias,
        compiler_params=pltpu.CompilerParams(vmem_limit_bytes=32 * MIB),
        cost_estimate=pl.CostEstimate(
            flops=2 * depth * (depth + channels) * TILE * n,
            bytes_accessed=6 * depth * TILE * n + 2 * depth * depth,
            transcendentals=depth * TILE * n,
        ),
        name="forward",
    )(table, *args)


def pair_kernel(table, own, side, *refs):
    near, (up, down, target, area), outs = refs[:4], refs[4:8], refs[8:]
    own_out, side_out, *near_outs = outs
    members = len(SLOTS)
    across = 0.95 / (members * (members - 1))
    channels = own.shape[0]
    for lane in range(0, TILE, 128):
        cols = slice(lane, lane + 128)
        weight = area[:, cols]
        second = lane >= HALF
        far, at = (down if second else up), lane % HALF
        halves = [slice(i * HALF + at, i * HALF + at + 128) for i in range(2)]
        tail = slice(TILE + at, TILE + at + 128)
        for low in range(0, channels, 8):
            rows = slice(low, min(low + 8, channels))
            p = [r[rows, cols] for r in (own, side, *near)] + [far[rows, h] for h in halves]
            t = target[rows, cols].astype(F32)
            total = [None] * members
            for a in range(members):
                for b in range(a + 1, members):
                    s = smooth(p[a] - p[b])
                    total[a] = s if total[a] is None else total[a] + s
                    total[b] = -s if total[b] is None else total[b] - s
            for a in range(members):
                g = weight * (smooth(p[a] - t) * (1.0 / members) - across * total[a])
                g = g.astype(BF16).astype(F32)
                if a < 6:
                    outs[a][rows, cols] = g
                else:
                    near_outs[2 * (a - 6) + second][rows, tail] = g


def pairs(me, own, side, near, relayed, target, area):
    channels = own.shape[0]
    fixed = pl.BlockSpec(memory_space=pltpu.VMEM)
    whole = pl.BlockSpec((channels, TILE), lambda g, t: (0, 0))
    return pl.pallas_call(
        pair_kernel,
        grid_spec=pltpu.PrefetchScalarGridSpec(
            num_scalar_prefetch=1,
            grid=(1,),
            in_specs=[whole]
            + [fixed] * 7
            + [
                pl.BlockSpec((channels, TILE), lambda g, t: (0, t[0])),
                pl.BlockSpec((1, TILE), lambda g, t: (0, t[0])),
            ],
            out_specs=[whole] + [fixed] * 5,
        ),
        out_shape=[pltpu.HBM((channels, TILE), F32), pltpu.VMEM((channels, TILE), F32)]
        + [pltpu.VMEM((channels, TILE + HALF), F32)] * 4,
        compiler_params=pltpu.CompilerParams(vmem_limit_bytes=16 * MIB),
        cost_estimate=pl.CostEstimate(
            flops=36 * 6 * channels * TILE,
            bytes_accessed=64 * channels * TILE,
            transcendentals=36 * channels * TILE,
        ),
        name="pairs",
    )(me, in_hbm(own), *map(in_vmem, (side, *near, *relayed)), target, area)


def backward_kernel(part, info, *refs):
    first, last, slots = part
    refs = list(refs)
    take = lambda k: [refs.pop(0) for _ in range(k)]
    grads = take(2 if last else len(slots))
    x_hbm, hidden, slope, ow = take(4)
    up_in, out_in, _ = (None, None, None) if first else take(3)
    grad = refs.pop(0)
    if last:
        away, keep, pg, x, up, out, sem = refs
    else:
        up, out, pg, x, sem = refs
    block = pl.program_id(0)
    channels, wide = pg.shape

    def fetch(i):
        tile = pl.ds(pl.multiple_of(info[1 + SLOTS.index(slots[i])] * TILE, TILE), TILE)
        place = slice(i * TILE, (i + 1) * TILE)
        return pltpu.make_async_copy(x_hbm.at[:, tile], x.at[:, place], sem.at[i])

    @pl.when(block == 0)
    def _():
        for i in range(len(slots)):
            fetch(i).start()
        for i in range(len(slots)):
            if last:
                for k, ref in enumerate(grads):
                    low = i * TILE + k * HALF
                    pg[:, low : low + HALF] = ref[:, i * HALF : (i + 1) * HALF].astype(BF16)
            else:
                pg[:, i * TILE : (i + 1) * TILE] = grads[i][:, :TILE].astype(BF16)

    for low in range(0, wide, ROWS):
        cols = slice(low, low + ROWS)
        hg = mm(ow[...], pg[:, cols], 1, 0)
        grad[:, cols] = (hg * slope[:, cols].astype(F32)).astype(BF16)
    part_out = mm(pg[...], hidden[...], 1, 1)

    @pl.when(block == 0)
    def _():
        for i in range(len(slots)):
            fetch(i).wait()

    part_up = mm(x[...], grad[...], 1, 1)
    if not first:
        part_out = part_out + out_in[0, :channels, :]
    shape = up.shape[-4:]
    part_up = part_up.reshape(shape)
    if not first:
        part_up = part_up + up_in[0]
    if not last:
        up[0] = part_up
        out[0, :channels, :] = part_out
    else:
        depth = keep.shape[2] - 128
        own = pl.ds(pl.multiple_of(block * ROWS, ROWS), ROWS)
        each = ROWS // 16
        rows = pl.ds(block * each, each)
        up[...] = part_up
        out[..., :channels] = part_out.T.reshape(each, 2, 8, channels)
        for ref, core in ((keep, info[0]), (away, 1 - info[0])):
            ref[:, :, own] = up[:, core]
            ref[rows, :, depth:] = out[:, core]


def backward(slots, info, grads, x, hidden, slope, ow, carried=None):
    first, last = carried is None, slots == FAR
    depth, cells = hidden.shape
    channels = ow.shape[1]
    chips, blocks, wide = depth // 16, depth // ROWS, len(slots) * TILE
    place = SLOTS.index(slots[0]) // len(slots)
    at = pl.BlockSpec((ROWS, wide), lambda b, t: (b, place))
    fixed = pl.BlockSpec(memory_space=pltpu.VMEM)
    any_spec = pl.BlockSpec(memory_space=pl.ANY)
    one = pl.BlockSpec((channels, TILE), lambda b, t: (0, 0))
    sums = [
        pl.BlockSpec((1, chips, 2, 8, ROWS), lambda b, t: (b, 0, 0, 0, 0)),
        pl.BlockSpec((1, 128, ROWS), lambda b, t: (b, 0, 0)),
    ]
    in_specs = [one if first and i == 0 else fixed for i in range(len(grads))]
    args = [in_hbm(g) if s is one else in_vmem(g) for g, s in zip(grads, in_specs)]
    in_specs += [any_spec, at, at, pl.BlockSpec((ROWS, channels), lambda b, t: (b, 0))]
    args += [in_hbm(x), in_hbm(hidden), in_hbm(slope), ow]
    out_shape, out_specs = [pltpu.HBM((depth, cells), BF16)], [at]
    scratch = [pltpu.VMEM((channels, wide), BF16), pltpu.VMEM((depth, wide), BF16)]
    alias = {}
    if not first:
        args += [in_hbm(carried[1]), in_hbm(carried[2]), carried[0]]
        in_specs += sums + [any_spec]
        alias = {len(args): 0}
    if last:
        out_shape += [pltpu.VMEM((chips, 8, depth + 128), F32)] * 2
        out_specs += [fixed, fixed]
        scratch += [pltpu.VMEM((chips, 2, 8, ROWS), F32), pltpu.VMEM((ROWS // 16, 2, 8, 128), F32)]
    else:
        out_shape += [
            pltpu.HBM((blocks, chips, 2, 8, ROWS), F32),
            pltpu.HBM((blocks, 128, ROWS), F32),
        ]
        out_specs += sums
    scratch += [pltpu.SemaphoreType.DMA((len(slots),))]
    return pl.pallas_call(
        functools.partial(backward_kernel, (first, last, slots)),
        grid_spec=pltpu.PrefetchScalarGridSpec(
            num_scalar_prefetch=1,
            grid=(blocks,),
            in_specs=in_specs,
            out_specs=out_specs,
            scratch_shapes=scratch,
        ),
        out_shape=out_shape,
        input_output_aliases=alias,
        compiler_params=pltpu.CompilerParams(vmem_limit_bytes=32 * MIB),
        cost_estimate=pl.CostEstimate(
            flops=2 * depth * (depth + 2 * channels) * wide,
            bytes_accessed=8 * depth * wide + 8 * depth * depth,
            transcendentals=0,
        ),
        name="backward",
    )(info, *args)


def feature_kernel(table, w, grad, out):
    out[0] = mm(w[...], grad[...], 1, 0).astype(BF16)


def feature_grad(table, w, grad):
    depth, cells = grad.shape
    return pl.pallas_call(
        feature_kernel,
        grid_spec=pltpu.PrefetchScalarGridSpec(
            num_scalar_prefetch=1,
            grid=(cells // TILE,),
            in_specs=[
                pl.BlockSpec((depth, depth), lambda g, t: (0, 0)),
                pl.BlockSpec((depth, TILE), lambda g, t: (0, g)),
            ],
            out_specs=pl.BlockSpec((1, depth, TILE), lambda g, t: (0, 0, t[g])),
        ),
        out_shape=jax.ShapeDtypeStruct((1, depth, cells), BF16),
        compiler_params=pltpu.CompilerParams(vmem_limit_bytes=24 * MIB),
        cost_estimate=pl.CostEstimate(
            flops=2 * depth * depth * cells,
            bytes_accessed=4 * depth * cells + 2 * depth * depth,
            transcendentals=0,
        ),
        name="feature_grad",
    )(table, in_hbm(w), in_hbm(grad))


def total_kernel(scale, parts, up, out):
    depth, channels = up.shape[1], out.shape[1]
    acc = parts[0]
    for c in range(1, parts.shape[0]):
        acc = acc + parts[c]
    acc = acc * scale
    up[...] = acc[:, :depth]
    out[...] = acc[:, depth : depth + channels]


def total(parts, depth, channels, scale):
    rows = parts.shape[1]
    return pl.pallas_call(
        functools.partial(total_kernel, scale),
        in_specs=[pl.BlockSpec(memory_space=pltpu.VMEM)],
        out_shape=[
            jax.ShapeDtypeStruct((rows, depth), F32),
            jax.ShapeDtypeStruct((rows, channels), F32),
        ],
        compiler_params=pltpu.CompilerParams(vmem_limit_bytes=16 * MIB),
        name="total",
    )(parts)


def spread(away, keep):
    swapped = lax.ppermute(away, "core", [(0, 1), (1, 0)])
    return lax.all_to_all(keep + swapped, CHIP, 0, 0, tiled=True)


def body(features, up_weight, out_weight, target, area):
    x = features[0]
    depth, cells = x.shape
    channels = out_weight.shape[1]
    owt = out_weight.T
    z, y = lax.axis_index("z"), lax.axis_index("ylo")
    core = lax.axis_index("core")

    def tile_of(slot):
        return 2 * lax.rem(z + slot[0], 4) + lax.bitwise_xor(y, slot[1])

    def table(slots):
        return jnp.stack([tile_of(s) for s in slots]).astype(jnp.int32)

    def plan(slots):
        return jnp.stack(
            [tile_of(s) for s in slots] + [jnp.int32(SLOTS.index(s)) for s in slots]
        ).astype(jnp.int32)

    def relay(blocks, step):
        passed = jnp.concatenate([block[:, TILE:] for block in blocks], axis=1)
        return lax.ppermute(passed, "z", [(i, (i + step) % 4) for i in range(4)])

    hidden, slope, *sent, wt, ow = forward(plan(NEAR + FAR), x, up_weight, owt)
    near = [lax.ppermute(block, MEMBER, route(s, False)) for s, block in zip(NEAR, sent)]
    hidden, slope, own, side = forward(plan(SIDE), x, wt, owt, (hidden, slope))
    side = lax.ppermute(side, MEMBER, route((0, 1), False))

    relayed = relay(near[0::2], 1), relay(near[1::2], -1)
    tiles = table(SLOTS)
    me = jnp.reshape(tile_of((0, 0)), (1,)).astype(jnp.int32)
    own, side, *sent = pairs(me, own, side, near, relayed, target, area[None, :])

    near = [lax.ppermute(block, MEMBER, route(s, True)) for s, block in zip(NEAR, sent)]
    side = lax.ppermute(side, MEMBER, route((0, 1), True))
    info = jnp.concatenate([jnp.reshape(core, (1,)).astype(jnp.int32), tiles])
    some = backward(SIDE, info, [own, side], x, hidden, slope, ow)
    relayed = relay(near[0::2], -1), relay(near[1::2], 1)
    more = backward(NEAR, info, near, x, hidden, slope, ow, some)
    pre_grad, away, keep = backward(FAR, info, relayed, x, hidden, slope, ow, more)
    parts = spread(away, keep)
    fgrad = feature_grad(tiles, up_weight, pre_grad)
    scale = 1.0 / math.sqrt(cells * lax.axis_size(SPACE) * lax.axis_size(MEMBER))
    up_grad, out_grad = total(parts, depth, channels, scale)
    return fgrad, up_grad, out_grad


def solution(mesh):
    fine = Mesh(mesh.devices.reshape(4, 2, 4, 2, 2), DEVICE)
    in_specs = (P(MEMBER, None, SPACE), P(), P(), P(None, SPACE), P(SPACE))
    out_specs = (P(MEMBER, None, SPACE), P(DEVICE, None), P(DEVICE, None))
    return jax.shard_map(body, mesh=fine, in_specs=in_specs, out_specs=out_specs, check_vma=False)
```

```python
import functools
import math

import jax
import jax.numpy as jnp
from jax import lax
from jax.experimental import pallas as pl
from jax.experimental.pallas import tpu as pltpu
from jax.sharding import Mesh
from jax.sharding import PartitionSpec as P


MEMBER = ("z", "ylo")
CHIP = ("z", "ylo", "x", "yhi")
SPACE = ("x", "yhi", "core")
DEVICE = ("z", "ylo", "x", "yhi", "core")

NEAR = ((1, 0), (3, 0), (1, 1), (3, 1))
SIDE = ((0, 0), (0, 1))
FAR = ((2, 0), (2, 1))
SLOTS = NEAR + SIDE + FAR

TILE = 512
SPAN = 1024
BLOCK = 512
HALF = 256
ROWS = 256
MIB = 1 << 20
BF16, F32 = jnp.bfloat16, jnp.float32


def route(slot, back):
    pairs = []
    for z in range(4):
        for y in range(2):
            here, there = 2 * z + y, 2 * ((z + slot[0]) % 4) + (y ^ slot[1])
            pairs.append((there, here) if back else (here, there))
    return pairs


def in_hbm(x):
    return pltpu.with_memory_space_constraint(x, pltpu.HBM)


def in_vmem(x):
    return pltpu.with_memory_space_constraint(x, pltpu.VMEM)


def smooth(diff):
    return diff * lax.rsqrt(diff * diff + 0.0625)


def mm(a, b, ca, cb):
    return lax.dot_general(a, b, (((ca,), (cb,)), ((), ())), preferred_element_type=F32)


def forward_kernel(first, tiles, *refs):
    if first:
        x, w, owt, hidden, slope, *preds, wt, ow = refs
    else:
        x, wt, owt, _, _, hidden, slope, *preds = refs
    step = pl.program_id(0)

    if first:

        @pl.when(step == 0)
        def _():
            for i in range(0, w.shape[0], ROWS):
                wt[:, i : i + ROWS] = (w[i : i + ROWS, :] * 0.5).T
            ow[...] = (owt[...] * 0.5).T

    h = mm(wt[...], x[...], 1, 0)
    u = jnp.tanh(h) + 1.0
    act = h * u
    hidden[...] = act.astype(BF16)
    slope[...] = (u + act * (2.0 - u)).astype(BF16)
    pred = mm(owt[...], hidden[...], 1, 0)
    if not first:
        for i, out in enumerate(preds):

            @pl.when(step == i)
            def _():
                out[...] = pred

        return
    for i, out in enumerate(preds):

        @pl.when(step == i)
        def _():
            out[:, :TILE] = pred

    for i in range(2):

        @pl.when(step == len(preds) + i)
        def _():
            preds[2 * i][:, TILE:] = pred[:, :HALF]
            preds[2 * i + 1][:, TILE:] = pred[:, HALF:]


def forward(table, x, w, owt, carried=None):
    first = carried is None
    depth, cells = x.shape
    channels = owt.shape[0]
    n = table.shape[0] // 2
    at_tile = pl.BlockSpec((depth, TILE), lambda g, t: (0, t[g]))
    at_slot = pl.BlockSpec((depth, TILE), lambda g, t: (0, t[n + g]))
    whole = lambda *s: pl.BlockSpec(s, lambda g, t: (0,) * len(s))
    fixed = pl.BlockSpec(memory_space=pltpu.VMEM)
    any_spec = pl.BlockSpec(memory_space=pl.ANY)
    act = pltpu.HBM((depth, cells), BF16)
    if first:
        out_shape = [act, act] + [pltpu.VMEM((channels, TILE + HALF), F32)] * 4
        out_specs = [at_slot, at_slot] + [fixed] * 4
    else:
        out_shape = [act, act, pltpu.HBM((channels, TILE), F32), pltpu.VMEM((channels, TILE), F32)]
        out_specs = [at_slot, at_slot, whole(channels, TILE), fixed]
    w_spec = whole(depth, depth) if first else fixed
    w = in_hbm(w) if first else in_vmem(w)
    args, in_specs = [in_hbm(x), w, in_hbm(owt)], [at_tile, w_spec, whole(channels, depth)]
    alias = {}
    if first:
        out_shape += [pltpu.VMEM((depth, depth), BF16), pltpu.HBM((depth, channels), BF16)]
        out_specs += [fixed, whole(depth, channels)]
    else:
        args += list(carried)
        in_specs += [any_spec, any_spec]
        alias = {4: 0, 5: 1}
    return pl.pallas_call(
        functools.partial(forward_kernel, first),
        grid_spec=pltpu.PrefetchScalarGridSpec(
            num_scalar_prefetch=1, grid=(n,), in_specs=in_specs, out_specs=out_specs
        ),
        out_shape=out_shape,
        input_output_aliases=alias,
        compiler_params=pltpu.CompilerParams(vmem_limit_bytes=32 * MIB),
        cost_estimate=pl.CostEstimate(
            flops=2 * depth * (depth + channels) * TILE * n,
            bytes_accessed=6 * depth * TILE * n + 2 * depth * depth,
            transcendentals=depth * TILE * n,
        ),
        name="forward",
    )(table, *args)


def pair_kernel(table, own, side, *refs):
    near, (up, down, target, area), outs = refs[:4], refs[4:8], refs[8:]
    own_out, side_out, *near_outs = outs
    members = len(SLOTS)
    across = 0.95 / (members * (members - 1))
    channels = own.shape[0]
    for lane in range(0, TILE, 128):
        cols = slice(lane, lane + 128)
        weight = area[:, cols]
        second = lane >= HALF
        far, at = (down if second else up), lane % HALF
        halves = [slice(i * HALF + at, i * HALF + at + 128) for i in range(2)]
        tail = slice(TILE + at, TILE + at + 128)
        for low in range(0, channels, 8):
            rows = slice(low, min(low + 8, channels))
            p = [r[rows, cols] for r in (own, side, *near)] + [far[rows, h] for h in halves]
            t = target[rows, cols].astype(F32)
            total = [None] * members
            for a in range(members):
                for b in range(a + 1, members):
                    s = smooth(p[a] - p[b])
                    total[a] = s if total[a] is None else total[a] + s
                    total[b] = -s if total[b] is None else total[b] - s
            for a in range(members):
                g = weight * (smooth(p[a] - t) * (1.0 / members) - across * total[a])
                g = g.astype(BF16).astype(F32)
                if a < 6:
                    outs[a][rows, cols] = g
                else:
                    near_outs[2 * (a - 6) + second][rows, tail] = g


def pairs(me, own, side, near, relayed, target, area):
    channels = own.shape[0]
    fixed = pl.BlockSpec(memory_space=pltpu.VMEM)
    whole = pl.BlockSpec((channels, TILE), lambda g, t: (0, 0))
    return pl.pallas_call(
        pair_kernel,
        grid_spec=pltpu.PrefetchScalarGridSpec(
            num_scalar_prefetch=1,
            grid=(1,),
            in_specs=[whole]
            + [fixed] * 7
            + [
                pl.BlockSpec((channels, TILE), lambda g, t: (0, t[0])),
                pl.BlockSpec((1, TILE), lambda g, t: (0, t[0])),
            ],
            out_specs=[whole] + [fixed] * 5,
        ),
        out_shape=[pltpu.HBM((channels, TILE), F32), pltpu.VMEM((channels, TILE), F32)]
        + [pltpu.VMEM((channels, TILE + HALF), F32)] * 4,
        compiler_params=pltpu.CompilerParams(vmem_limit_bytes=16 * MIB),
        cost_estimate=pl.CostEstimate(
            flops=36 * 6 * channels * TILE,
            bytes_accessed=64 * channels * TILE,
            transcendentals=36 * channels * TILE,
        ),
        name="pairs",
    )(me, in_hbm(own), *map(in_vmem, (side, *near, *relayed)), target, area)


def backward_kernel(info, *refs):
    near, own, side, relayed = refs[:4], refs[4], refs[5], refs[6:8]
    x_hbm, hidden, slope, ow, grad, away, keep, pg, x, up, out, sem = refs[8:]
    block, chunk = pl.program_id(0), pl.program_id(1)
    channels, wide = pg.shape[0], grad.shape[1]
    chunks, each = x.shape[1] // wide, wide // TILE

    def fetch(i):
        tile = pl.ds(pl.multiple_of(info[1 + i] * TILE, TILE), TILE)
        place = slice(i * TILE, (i + 1) * TILE)
        return pltpu.make_async_copy(x_hbm.at[:, tile], x.at[:, place], sem.at[i])

    @pl.when((block == 0) & (chunk == 0))
    def _():
        for i in range(len(SLOTS)):
            fetch(i).start()
        for i, ref in enumerate((*near, own, side)):
            pg[:, i * TILE : (i + 1) * TILE] = ref[:, :TILE].astype(BF16)
        for i in range(len(FAR)):
            for k, ref in enumerate(relayed):
                low = (6 + i) * TILE + k * HALF
                pg[:, low : low + HALF] = ref[:, i * HALF : (i + 1) * HALF].astype(BF16)

    for c in range(chunks):

        @pl.when((block == 0) & (chunk == c))
        def _():
            for i in range(c * each, (c + 1) * each):
                fetch(i).wait()

    span = pl.ds(pl.multiple_of(chunk * wide, wide), wide)
    pgt = pg[:, span]
    for low in range(0, wide, ROWS):
        cols = slice(low, low + ROWS)
        hg = mm(ow[...], pgt[:, cols], 1, 0)
        grad[:, cols] = (hg * slope[:, cols].astype(F32)).astype(BF16)
    opening = chunk == 0
    part_out = mm(pgt, hidden[...], 1, 1)
    out[:channels, :] = jnp.where(opening, 0.0, out[:channels, :]) + part_out
    part_up = mm(x[:, span], grad[...], 1, 1).reshape(up.shape)
    up[...] = jnp.where(opening, 0.0, up[...]) + part_up

    @pl.when(chunk == chunks - 1)
    def _():
        depth = keep.shape[2] - 128
        cols = pl.ds(pl.multiple_of(block * BLOCK, BLOCK), BLOCK)
        some = BLOCK // 16
        rows = pl.ds(block * some, some)
        for ref, core in ((keep, info[0]), (away, 1 - info[0])):
            ref[:, :, cols] = up[:, core]
        up[:some, :, :, :128] = out[...].T.reshape(some, 2, 8, 128)
        for ref, core in ((keep, info[0]), (away, 1 - info[0])):
            ref[rows, :, depth:] = up[:some, core, :, :128]


def backward(info, near, own, side, relayed, x, hidden, slope, ow):
    depth, cells = hidden.shape
    channels = ow.shape[1]
    chips, blocks = depth // 16, depth // BLOCK
    at = pl.BlockSpec((BLOCK, SPAN), lambda b, c, t: (b, c))
    fixed = pl.BlockSpec(memory_space=pltpu.VMEM)
    return pl.pallas_call(
        backward_kernel,
        grid_spec=pltpu.PrefetchScalarGridSpec(
            num_scalar_prefetch=1,
            grid=(blocks, cells // SPAN),
            in_specs=[fixed] * 4
            + [pl.BlockSpec((channels, TILE), lambda b, c, t: (0, 0))]
            + [fixed] * 3
            + [
                pl.BlockSpec(memory_space=pl.ANY),
                at,
                at,
                pl.BlockSpec((BLOCK, channels), lambda b, c, t: (b, 0)),
            ],
            out_specs=[at, fixed, fixed],
            scratch_shapes=[
                pltpu.VMEM((channels, cells), BF16),
                pltpu.VMEM((depth, cells), BF16),
                pltpu.VMEM((chips, 2, 8, BLOCK), F32),
                pltpu.VMEM((128, BLOCK), F32),
                pltpu.SemaphoreType.DMA((len(SLOTS),)),
            ],
        ),
        out_shape=[pltpu.HBM((depth, cells), BF16)]
        + [pltpu.VMEM((chips, 8, depth + 128), F32)] * 2,
        compiler_params=pltpu.CompilerParams(vmem_limit_bytes=40 * MIB),
        cost_estimate=pl.CostEstimate(
            flops=2 * depth * (depth + 2 * channels) * cells,
            bytes_accessed=8 * depth * cells + 4 * depth * depth,
            transcendentals=0,
        ),
        name="backward",
    )(
        info,
        *map(in_vmem, near),
        in_hbm(own),
        *map(in_vmem, (side, *relayed)),
        in_hbm(x),
        in_hbm(hidden),
        in_hbm(slope),
        in_hbm(ow),
    )


def feature_kernel(table, w, grad, out):
    out[0] = mm(w[...], grad[...], 1, 0).astype(BF16)


def feature_grad(table, w, grad):
    depth, cells = grad.shape
    return pl.pallas_call(
        feature_kernel,
        grid_spec=pltpu.PrefetchScalarGridSpec(
            num_scalar_prefetch=1,
            grid=(cells // TILE,),
            in_specs=[
                pl.BlockSpec((depth, depth), lambda g, t: (0, 0)),
                pl.BlockSpec((depth, TILE), lambda g, t: (0, g)),
            ],
            out_specs=pl.BlockSpec((1, depth, TILE), lambda g, t: (0, 0, t[g])),
        ),
        out_shape=jax.ShapeDtypeStruct((1, depth, cells), BF16),
        compiler_params=pltpu.CompilerParams(vmem_limit_bytes=24 * MIB),
        cost_estimate=pl.CostEstimate(
            flops=2 * depth * depth * cells,
            bytes_accessed=4 * depth * cells + 2 * depth * depth,
            transcendentals=0,
        ),
        name="feature_grad",
    )(table, in_hbm(w), in_hbm(grad))


def total_kernel(scale, parts, up, out):
    depth, channels = up.shape[1], out.shape[1]
    acc = parts[0]
    for c in range(1, parts.shape[0]):
        acc = acc + parts[c]
    acc = acc * scale
    up[...] = acc[:, :depth]
    out[...] = acc[:, depth : depth + channels]


def total(parts, depth, channels, scale):
    rows = parts.shape[1]
    return pl.pallas_call(
        functools.partial(total_kernel, scale),
        in_specs=[pl.BlockSpec(memory_space=pltpu.VMEM)],
        out_shape=[
            jax.ShapeDtypeStruct((rows, depth), F32),
            jax.ShapeDtypeStruct((rows, channels), F32),
        ],
        compiler_params=pltpu.CompilerParams(vmem_limit_bytes=16 * MIB),
        name="total",
    )(parts)


def spread(away, keep):
    swapped = lax.ppermute(away, "core", [(0, 1), (1, 0)])
    return lax.all_to_all(keep + swapped, CHIP, 0, 0, tiled=True)


def body(features, up_weight, out_weight, target, area):
    x = features[0]
    depth, cells = x.shape
    channels = out_weight.shape[1]
    owt = out_weight.T
    z, y = lax.axis_index("z"), lax.axis_index("ylo")
    core = lax.axis_index("core")

    def tile_of(slot):
        return 2 * lax.rem(z + slot[0], 4) + lax.bitwise_xor(y, slot[1])

    def table(slots):
        return jnp.stack([tile_of(s) for s in slots]).astype(jnp.int32)

    def plan(slots):
        return jnp.stack(
            [tile_of(s) for s in slots] + [jnp.int32(SLOTS.index(s)) for s in slots]
        ).astype(jnp.int32)

    def relay(blocks, step):
        passed = jnp.concatenate([block[:, TILE:] for block in blocks], axis=1)
        return lax.ppermute(passed, "z", [(i, (i + step) % 4) for i in range(4)])

    hidden, slope, *sent, wt, ow = forward(plan(NEAR + FAR), x, up_weight, owt)
    near = [lax.ppermute(block, MEMBER, route(s, False)) for s, block in zip(NEAR, sent)]
    hidden, slope, own, side = forward(plan(SIDE), x, wt, owt, (hidden, slope))
    side = lax.ppermute(side, MEMBER, route((0, 1), False))

    relayed = relay(near[0::2], 1), relay(near[1::2], -1)
    tiles = table(SLOTS)
    me = jnp.reshape(tile_of((0, 0)), (1,)).astype(jnp.int32)
    own, side, *sent = pairs(me, own, side, near, relayed, target, area[None, :])

    near = [lax.ppermute(block, MEMBER, route(s, True)) for s, block in zip(NEAR, sent)]
    side = lax.ppermute(side, MEMBER, route((0, 1), True))
    info = jnp.concatenate([jnp.reshape(core, (1,)).astype(jnp.int32), tiles])
    relayed = relay(near[0::2], -1), relay(near[1::2], 1)
    pre_grad, away, keep = backward(info, near, own, side, relayed, x, hidden, slope, ow)
    parts = spread(away, keep)
    fgrad = feature_grad(tiles, up_weight, pre_grad)
    scale = 1.0 / math.sqrt(cells * lax.axis_size(SPACE) * lax.axis_size(MEMBER))
    up_grad, out_grad = total(parts, depth, channels, scale)
    return fgrad, up_grad, out_grad


def solution(mesh):
    fine = Mesh(mesh.devices.reshape(4, 2, 4, 2, 2), DEVICE)
    in_specs = (P(MEMBER, None, SPACE), P(), P(), P(None, SPACE), P(SPACE))
    out_specs = (P(MEMBER, None, SPACE), P(DEVICE, None), P(DEVICE, None))
    return jax.shard_map(body, mesh=fine, in_specs=in_specs, out_specs=out_specs, check_vma=False)
```

```python
import functools
import math

import jax
import jax.numpy as jnp
from jax import lax
from jax.experimental import pallas as pl
from jax.experimental.pallas import tpu as pltpu
from jax.sharding import Mesh
from jax.sharding import PartitionSpec as P


MEMBER = ("z", "ylo")
CHIP = ("z", "ylo", "x", "yhi")
SPACE = ("x", "yhi", "core")
DEVICE = ("z", "ylo", "x", "yhi", "core")

NEAR = ((1, 0), (3, 0), (1, 1), (3, 1))
SIDE = ((0, 0), (0, 1))
FAR = ((2, 0), (2, 1))
SLOTS = NEAR + SIDE + FAR

TILE = 512
SPAN = 1024
BLOCK = 512
HALF = 256
ROWS = 256
MIB = 1 << 20
BF16, F32 = jnp.bfloat16, jnp.float32


def route(slot, back):
    pairs = []
    for z in range(4):
        for y in range(2):
            here, there = 2 * z + y, 2 * ((z + slot[0]) % 4) + (y ^ slot[1])
            pairs.append((there, here) if back else (here, there))
    return pairs


def in_hbm(x):
    return pltpu.with_memory_space_constraint(x, pltpu.HBM)


def in_vmem(x):
    return pltpu.with_memory_space_constraint(x, pltpu.VMEM)


def smooth(diff):
    return diff * lax.rsqrt(diff * diff + 0.0625)


def mm(a, b, ca, cb):
    return lax.dot_general(a, b, (((ca,), (cb,)), ((), ())), preferred_element_type=F32)


def forward_kernel(first, side, table, *refs):
    if first:
        x, w, owt, hidden, slope, *preds, wt, ow = refs
    else:
        x, wt, owt, _, _, hidden, slope, *preds = refs
    step = pl.program_id(0)

    if first:

        @pl.when(step == 0)
        def _():
            for i in range(0, w.shape[0], ROWS):
                wt[:, i : i + ROWS] = (w[i : i + ROWS, :] * 0.5).T
            ow[...] = (owt[...] * 0.5).T

    h = mm(wt[...], x[...], 1, 0)
    u = jnp.tanh(h) + 1.0
    act = h * u
    hidden[0] = act.astype(BF16)
    slope[0] = (u + act * (2.0 - u)).astype(BF16)
    pred = mm(owt[...], hidden[0], 1, 0)
    for i, out in enumerate(preds):

        @pl.when(step == i)
        def _():
            out[:, :TILE] = pred

    if not side:

        @pl.when(step == 2)
        def _():
            preds[0][:, TILE:] = pred[:, :HALF]
            preds[1][:, TILE:] = pred[:, HALF:]


def forward(slots, tiles, x, w, owt, carried=None):
    first, side = carried is None, slots == SIDE
    depth, cells = x.shape
    channels = owt.shape[0]
    n = len(slots)
    table = jnp.stack([tiles[s] for s in slots] + [jnp.int32(SLOTS.index(s)) for s in slots])
    at_tile = pl.BlockSpec((depth, TILE), lambda g, t: (0, t[g]))
    at_slot = pl.BlockSpec((1, depth, TILE), lambda g, t: (t[n + g], 0, 0))
    whole = lambda *s: pl.BlockSpec(s, lambda g, t: (0,) * len(s))
    fixed = pl.BlockSpec(memory_space=pltpu.VMEM)
    any_spec = pl.BlockSpec(memory_space=pl.ANY)
    act = pltpu.HBM((len(SLOTS), depth, TILE), BF16)
    if side:
        out_shape = [act, act, pltpu.HBM((channels, TILE), F32), pltpu.VMEM((channels, TILE), F32)]
        out_specs = [at_slot, at_slot, whole(channels, TILE), fixed]
    else:
        out_shape = [act, act] + [pltpu.VMEM((channels, TILE + HALF), F32)] * 2
        out_specs = [at_slot, at_slot, fixed, fixed]
    w_spec = whole(depth, depth) if first else fixed
    w = in_hbm(w) if first else in_vmem(w)
    args, in_specs = [in_hbm(x), w, in_hbm(owt)], [at_tile, w_spec, whole(channels, depth)]
    alias = {}
    if first:
        out_shape += [pltpu.VMEM((depth, depth), BF16), pltpu.HBM((depth, channels), BF16)]
        out_specs += [fixed, whole(depth, channels)]
    else:
        args += list(carried)
        in_specs += [any_spec, any_spec]
        alias = {4: 0, 5: 1}
    return pl.pallas_call(
        functools.partial(forward_kernel, first, side),
        grid_spec=pltpu.PrefetchScalarGridSpec(
            num_scalar_prefetch=1, grid=(n,), in_specs=in_specs, out_specs=out_specs
        ),
        out_shape=out_shape,
        input_output_aliases=alias,
        compiler_params=pltpu.CompilerParams(vmem_limit_bytes=32 * MIB),
        cost_estimate=pl.CostEstimate(
            flops=2 * depth * (depth + channels) * TILE * n,
            bytes_accessed=6 * depth * TILE * n + 2 * depth * depth,
            transcendentals=depth * TILE * n,
        ),
        name="forward",
    )(table, *args)


def pair_kernel(table, own, side, *refs):
    near, (up, down, target, area), outs = refs[:4], refs[4:8], refs[8:]
    own_out, side_out, *near_outs = outs
    members = len(SLOTS)
    across = 0.95 / (members * (members - 1))
    channels = own.shape[0]
    for lane in range(0, TILE, 128):
        cols = slice(lane, lane + 128)
        weight = area[:, cols]
        second = lane >= HALF
        far, at = (down if second else up), lane % HALF
        halves = [slice(i * HALF + at, i * HALF + at + 128) for i in range(2)]
        tail = slice(TILE + at, TILE + at + 128)
        for low in range(0, channels, 8):
            rows = slice(low, min(low + 8, channels))
            p = [r[rows, cols] for r in (own, side, *near)] + [far[rows, h] for h in halves]
            t = target[rows, cols].astype(F32)
            total = [None] * members
            for a in range(members):
                for b in range(a + 1, members):
                    s = smooth(p[a] - p[b])
                    total[a] = s if total[a] is None else total[a] + s
                    total[b] = -s if total[b] is None else total[b] - s
            for a in range(members):
                g = weight * (smooth(p[a] - t) * (1.0 / members) - across * total[a])
                g = g.astype(BF16).astype(F32)
                if a < 6:
                    outs[a][rows, cols] = g
                else:
                    near_outs[2 * (a - 6) + second][rows, tail] = g


def pairs(me, own, side, near, relayed, target, area):
    channels = own.shape[0]
    fixed = pl.BlockSpec(memory_space=pltpu.VMEM)
    whole = pl.BlockSpec((channels, TILE), lambda g, t: (0, 0))
    return pl.pallas_call(
        pair_kernel,
        grid_spec=pltpu.PrefetchScalarGridSpec(
            num_scalar_prefetch=1,
            grid=(1,),
            in_specs=[whole]
            + [fixed] * 7
            + [
                pl.BlockSpec((channels, TILE), lambda g, t: (0, t[0])),
                pl.BlockSpec((1, TILE), lambda g, t: (0, t[0])),
            ],
            out_specs=[whole] + [fixed] * 5,
        ),
        out_shape=[pltpu.HBM((channels, TILE), F32), pltpu.VMEM((channels, TILE), F32)]
        + [pltpu.VMEM((channels, TILE + HALF), F32)] * 4,
        compiler_params=pltpu.CompilerParams(vmem_limit_bytes=16 * MIB),
        cost_estimate=pl.CostEstimate(
            flops=36 * 6 * channels * TILE,
            bytes_accessed=64 * channels * TILE,
            transcendentals=36 * channels * TILE,
        ),
        name="pairs",
    )(me, in_hbm(own), *map(in_vmem, (side, *near, *relayed)), target, area)


def backward_kernel(info, *refs):
    near, own, side, relayed = refs[:4], refs[4], refs[5], refs[6:8]
    x_hbm, hidden, slope, ow, grad, away, keep, pg, x, up, out, sem = refs[8:]
    block, chunk = pl.program_id(0), pl.program_id(1)
    channels, each = pg.shape[0], grad.shape[0]
    wide, chunks = each * TILE, len(SLOTS) // each

    def fetch(i):
        tile = pl.ds(pl.multiple_of(info[1 + i] * TILE, TILE), TILE)
        place = slice(i * TILE, (i + 1) * TILE)
        return pltpu.make_async_copy(x_hbm.at[:, tile], x.at[:, place], sem.at[i])

    @pl.when((block == 0) & (chunk == 0))
    def _():
        for i in range(len(SLOTS)):
            fetch(i).start()
        for i, ref in enumerate((*near, own, side)):
            pg[:, i * TILE : (i + 1) * TILE] = ref[:, :TILE].astype(BF16)
        for i in range(len(FAR)):
            for k, ref in enumerate(relayed):
                low = (6 + i) * TILE + k * HALF
                pg[:, low : low + HALF] = ref[:, i * HALF : (i + 1) * HALF].astype(BF16)

    for c in range(chunks):

        @pl.when((block == 0) & (chunk == c))
        def _():
            for i in range(c * each, (c + 1) * each):
                fetch(i).wait()

    span = pl.ds(pl.multiple_of(chunk * wide, wide), wide)
    pgt = pg[:, span]
    for low in range(0, wide, ROWS):
        hg = mm(ow[...], pgt[:, low : low + ROWS], 1, 0)
        i, cols = low // TILE, slice(low % TILE, low % TILE + ROWS)
        grad[i, :, cols] = (hg * slope[i, :, cols].astype(F32)).astype(BF16)
    join = lambda ref: jnp.concatenate([ref[i] for i in range(each)], axis=1)
    opening = chunk == 0
    part_out = mm(pgt, join(hidden), 1, 1)
    out[:channels, :] = jnp.where(opening, 0.0, out[:channels, :]) + part_out
    part_up = mm(x[:, span], join(grad), 1, 1).reshape(up.shape)
    up[...] = jnp.where(opening, 0.0, up[...]) + part_up

    @pl.when(chunk == chunks - 1)
    def _():
        depth = keep.shape[2] - 128
        cols = pl.ds(pl.multiple_of(block * BLOCK, BLOCK), BLOCK)
        some = BLOCK // 16
        rows = pl.ds(block * some, some)
        for ref, core in ((keep, info[0]), (away, 1 - info[0])):
            ref[:, :, cols] = up[:, core]
        up[:some, :, :, :128] = out[...].T.reshape(some, 2, 8, 128)
        for ref, core in ((keep, info[0]), (away, 1 - info[0])):
            ref[rows, :, depth:] = up[:some, core, :, :128]


def backward(info, near, own, side, relayed, x, hidden, slope, ow):
    depth, cells = x.shape
    channels = ow.shape[1]
    chips, blocks = depth // 16, depth // BLOCK
    at = pl.BlockSpec((SPAN // TILE, BLOCK, TILE), lambda b, c, t: (c, b, 0))
    fixed = pl.BlockSpec(memory_space=pltpu.VMEM)
    return pl.pallas_call(
        backward_kernel,
        grid_spec=pltpu.PrefetchScalarGridSpec(
            num_scalar_prefetch=1,
            grid=(blocks, cells // SPAN),
            in_specs=[fixed] * 4
            + [pl.BlockSpec((channels, TILE), lambda b, c, t: (0, 0))]
            + [fixed] * 3
            + [
                pl.BlockSpec(memory_space=pl.ANY),
                at,
                at,
                pl.BlockSpec((BLOCK, channels), lambda b, c, t: (b, 0)),
            ],
            out_specs=[at, fixed, fixed],
            scratch_shapes=[
                pltpu.VMEM((channels, cells), BF16),
                pltpu.VMEM((depth, cells), BF16),
                pltpu.VMEM((chips, 2, 8, BLOCK), F32),
                pltpu.VMEM((128, BLOCK), F32),
                pltpu.SemaphoreType.DMA((len(SLOTS),)),
            ],
        ),
        out_shape=[pltpu.HBM(hidden.shape, BF16)]
        + [pltpu.VMEM((chips, 8, depth + 128), F32)] * 2,
        compiler_params=pltpu.CompilerParams(vmem_limit_bytes=40 * MIB),
        cost_estimate=pl.CostEstimate(
            flops=2 * depth * (depth + 2 * channels) * cells,
            bytes_accessed=8 * depth * cells + 4 * depth * depth,
            transcendentals=0,
        ),
        name="backward",
    )(
        info,
        *map(in_vmem, near),
        in_hbm(own),
        *map(in_vmem, (side, *relayed)),
        in_hbm(x),
        in_hbm(hidden),
        in_hbm(slope),
        in_hbm(ow),
    )


def feature_kernel(table, w, grad, out):
    out[0] = mm(w[...], grad[0], 1, 0).astype(BF16)


def feature_grad(table, w, grad):
    depth, cells = grad.shape[1], grad.shape[0] * TILE
    return pl.pallas_call(
        feature_kernel,
        grid_spec=pltpu.PrefetchScalarGridSpec(
            num_scalar_prefetch=1,
            grid=(cells // TILE,),
            in_specs=[
                pl.BlockSpec((depth, depth), lambda g, t: (0, 0)),
                pl.BlockSpec((1, depth, TILE), lambda g, t: (g, 0, 0)),
            ],
            out_specs=pl.BlockSpec((1, depth, TILE), lambda g, t: (0, 0, t[g])),
        ),
        out_shape=jax.ShapeDtypeStruct((1, depth, cells), BF16),
        compiler_params=pltpu.CompilerParams(vmem_limit_bytes=24 * MIB),
        cost_estimate=pl.CostEstimate(
            flops=2 * depth * depth * cells,
            bytes_accessed=4 * depth * cells + 2 * depth * depth,
            transcendentals=0,
        ),
        name="feature_grad",
    )(table, in_hbm(w), in_hbm(grad))


def total_kernel(scale, parts, up, out):
    depth, channels = up.shape[1], out.shape[1]
    acc = parts[0]
    for c in range(1, parts.shape[0]):
        acc = acc + parts[c]
    acc = acc * scale
    up[...] = acc[:, :depth]
    out[...] = acc[:, depth : depth + channels]


def total(parts, depth, channels, scale):
    rows = parts.shape[1]
    return pl.pallas_call(
        functools.partial(total_kernel, scale),
        in_specs=[pl.BlockSpec(memory_space=pltpu.VMEM)],
        out_shape=[
            jax.ShapeDtypeStruct((rows, depth), F32),
            jax.ShapeDtypeStruct((rows, channels), F32),
        ],
        compiler_params=pltpu.CompilerParams(vmem_limit_bytes=16 * MIB),
        name="total",
    )(parts)


def spread(away, keep):
    swapped = lax.ppermute(away, "core", [(0, 1), (1, 0)])
    return lax.all_to_all(keep + swapped, CHIP, 0, 0, tiled=True)


def body(features, up_weight, out_weight, target, area):
    x = features[0]
    depth, cells = x.shape
    channels = out_weight.shape[1]
    owt = out_weight.T
    z, y = lax.axis_index("z"), lax.axis_index("ylo")
    core = lax.axis_index("core")

    tiles = {
        s: (2 * lax.rem(z + s[0], 4) + lax.bitwise_xor(y, s[1])).astype(jnp.int32) for s in SLOTS
    }

    def relay(blocks, step):
        passed = jnp.concatenate([block[:, TILE:] for block in blocks], axis=1)
        return lax.ppermute(passed, "z", [(i, (i + step) % 4) for i in range(4)])

    hidden, slope, *sent, wt, ow = forward(NEAR[:2] + FAR[:1], tiles, x, up_weight, owt)
    near = [lax.ppermute(block, MEMBER, route(s, False)) for s, block in zip(NEAR, sent)]
    hidden, slope, *sent = forward(NEAR[2:] + FAR[1:], tiles, x, wt, owt, (hidden, slope))
    near += [lax.ppermute(block, MEMBER, route(s, False)) for s, block in zip(NEAR[2:], sent)]
    hidden, slope, own, side = forward(SIDE, tiles, x, wt, owt, (hidden, slope))
    side = lax.ppermute(side, MEMBER, route((0, 1), False))

    relayed = relay(near[0::2], 1), relay(near[1::2], -1)
    me = jnp.reshape(tiles[0, 0], (1,))
    tiles = jnp.stack([tiles[s] for s in SLOTS])
    own, side, *sent = pairs(me, own, side, near, relayed, target, area[None, :])

    near = [lax.ppermute(block, MEMBER, route(s, True)) for s, block in zip(NEAR, sent)]
    side = lax.ppermute(side, MEMBER, route((0, 1), True))
    info = jnp.concatenate([jnp.reshape(core, (1,)).astype(jnp.int32), tiles])
    relayed = relay(near[0::2], -1), relay(near[1::2], 1)
    pre_grad, away, keep = backward(info, near, own, side, relayed, x, hidden, slope, ow)
    parts = spread(away, keep)
    fgrad = feature_grad(tiles, up_weight, pre_grad)
    scale = 1.0 / math.sqrt(cells * lax.axis_size(SPACE) * lax.axis_size(MEMBER))
    up_grad, out_grad = total(parts, depth, channels, scale)
    return fgrad, up_grad, out_grad


def solution(mesh):
    fine = Mesh(mesh.devices.reshape(4, 2, 4, 2, 2), DEVICE)
    in_specs = (P(MEMBER, None, SPACE), P(), P(), P(None, SPACE), P(SPACE))
    out_specs = (P(MEMBER, None, SPACE), P(DEVICE, None), P(DEVICE, None))
    return jax.shard_map(body, mesh=fine, in_specs=in_specs, out_specs=out_specs, check_vma=False)
```

```python
import functools
import math

import jax
import jax.numpy as jnp
from jax import lax
from jax.experimental import pallas as pl
from jax.experimental.pallas import tpu as pltpu
from jax.sharding import Mesh
from jax.sharding import PartitionSpec as P


MEMBER = ("z", "ylo")
CHIP = ("z", "ylo", "x", "yhi")
SPACE = ("x", "yhi", "core")
DEVICE = ("z", "ylo", "x", "yhi", "core")

NEAR = ((1, 0), (3, 0), (1, 1), (3, 1))
SIDE = ((0, 0), (0, 1))
FAR = ((2, 0), (2, 1))
SLOTS = NEAR + SIDE + FAR
FIRST = ((2, 1), (2, 0), (1, 1), (3, 1), (0, 1))
SECOND = ((1, 0), (3, 0), (0, 0))
ORDER = FIRST + SECOND

TILE = 512
SPAN = 1024
BLOCK = 512
HALF = 256
ROWS = 256
MIB = 1 << 20
BF16, F32 = jnp.bfloat16, jnp.float32


def route(slot, back):
    pairs = []
    for z in range(4):
        for y in range(2):
            here, there = 2 * z + y, 2 * ((z + slot[0]) % 4) + (y ^ slot[1])
            pairs.append((there, here) if back else (here, there))
    return pairs


def in_hbm(x):
    return pltpu.with_memory_space_constraint(x, pltpu.HBM)


def in_vmem(x):
    return pltpu.with_memory_space_constraint(x, pltpu.VMEM)


def smooth(diff):
    return diff * lax.rsqrt(diff * diff + 0.0625)


def mm(a, b, ca, cb):
    return lax.dot_general(a, b, (((ca,), (cb,)), ((), ())), preferred_element_type=F32)


def forward_kernel(first, info, *refs):
    if first:
        x, w, owt, hidden, slope, *preds, wt, ow = refs
    else:
        x, wt, owt, _, _, hidden, slope, *preds = refs
    step = pl.program_id(0)

    if first:

        @pl.when(step == 0)
        def _():
            for i in range(0, w.shape[0], ROWS):
                wt[:, i : i + ROWS] = (w[i : i + ROWS, :] * 0.5).T
            ow[...] = (owt[...] * 0.5).T

    slot = info[17 + (0 if first else len(FIRST)) + step]
    h = mm(wt[...], x[...], 1, 0)
    u = jnp.tanh(h) + 1.0
    act = h * u
    rounded = act.astype(BF16)
    hidden[slot] = rounded
    slope[slot] = (u + act * (2.0 - u)).astype(BF16)
    pred = mm(owt[...], rounded, 1, 0)
    for i, out in enumerate(preds):

        @pl.when(step == i)
        def _():
            out[...] = pred


def forward(info, x, w, owt, carried=None):
    first = carried is None
    depth, _ = x.shape
    channels = owt.shape[0]
    n, base = (len(FIRST), 0) if first else (len(SECOND), len(FIRST))
    at_tile = pl.BlockSpec((depth, TILE), lambda g, t: (0, t[9 + base + g]))
    whole = lambda *s: pl.BlockSpec(s, lambda g, t: (0,) * len(s))
    fixed = pl.BlockSpec(memory_space=pltpu.VMEM)
    act = pltpu.VMEM((len(SLOTS), depth, TILE), BF16)
    out_shape = [act, act] + [pltpu.VMEM((channels, TILE), F32)] * n
    out_specs = [fixed, fixed] + [fixed] * n
    w_spec = whole(depth, depth) if first else fixed
    w = in_hbm(w) if first else in_vmem(w)
    args, in_specs = [in_hbm(x), w, in_hbm(owt)], [at_tile, w_spec, whole(channels, depth)]
    alias = {}
    if first:
        out_shape += [pltpu.VMEM((depth, depth), BF16), pltpu.HBM((depth, channels), BF16)]
        out_specs += [fixed, whole(depth, channels)]
    else:
        out_shape[-1] = pltpu.HBM((channels, TILE), F32)
        out_specs[-1] = whole(channels, TILE)
        args += map(in_vmem, carried)
        in_specs += [fixed, fixed]
        alias = {4: 0, 5: 1}
    return pl.pallas_call(
        functools.partial(forward_kernel, first),
        grid_spec=pltpu.PrefetchScalarGridSpec(
            num_scalar_prefetch=1, grid=(n,), in_specs=in_specs, out_specs=out_specs
        ),
        out_shape=out_shape,
        input_output_aliases=alias,
        compiler_params=pltpu.CompilerParams(vmem_limit_bytes=16 * MIB),
        cost_estimate=pl.CostEstimate(
            flops=2 * depth * (depth + channels) * TILE * n,
            bytes_accessed=6 * depth * TILE * n + 2 * depth * depth,
            transcendentals=depth * TILE * n,
        ),
        name="forward",
    )(info, *args)


def pair_kernel(info, *refs):
    preds, (target, area), outs = refs[:8], refs[8:10], refs[10:]
    own_out, side_out, *near_outs = outs
    members = len(SLOTS)
    across = 0.95 / (members * (members - 1))
    channels = target.shape[0]
    for lane in range(0, TILE, 128):
        cols = slice(lane, lane + 128)
        weight = area[:, cols]
        second = lane >= HALF
        at = lane % HALF
        tail = slice(TILE + at, TILE + at + 128)
        for low in range(0, channels, 8):
            rows = slice(low, min(low + 8, channels))
            p = [r[rows, cols] for r in preds]
            t = target[rows, cols].astype(F32)
            total = [None] * members
            for a in range(members):
                for b in range(a + 1, members):
                    s = smooth(p[a] - p[b])
                    total[a] = s if total[a] is None else total[a] + s
                    total[b] = -s if total[b] is None else total[b] - s
            for a in range(members):
                g = weight * (smooth(p[a] - t) * (1.0 / members) - across * total[a])
                g = g.astype(BF16).astype(F32)
                if a < 6:
                    outs[a][rows, cols] = g
                else:
                    near_outs[2 * (a - 6) + second][rows, tail] = g


def pairs(info, preds, target, area):
    channels = target.shape[0]
    me = 1 + SLOTS.index((0, 0))
    fixed = pl.BlockSpec(memory_space=pltpu.VMEM)
    whole = pl.BlockSpec((channels, TILE), lambda g, t: (0, 0))
    return pl.pallas_call(
        pair_kernel,
        grid_spec=pltpu.PrefetchScalarGridSpec(
            num_scalar_prefetch=1,
            grid=(1,),
            in_specs=[whole]
            + [fixed] * 7
            + [
                pl.BlockSpec((channels, TILE), lambda g, t: (0, t[me])),
                pl.BlockSpec((1, TILE), lambda g, t: (0, t[me])),
            ],
            out_specs=[whole] + [fixed] * 5,
        ),
        out_shape=[pltpu.HBM((channels, TILE), F32), pltpu.VMEM((channels, TILE), F32)]
        + [pltpu.VMEM((channels, TILE + HALF), F32)] * 4,
        compiler_params=pltpu.CompilerParams(vmem_limit_bytes=16 * MIB),
        cost_estimate=pl.CostEstimate(
            flops=36 * 6 * channels * TILE,
            bytes_accessed=64 * channels * TILE,
            transcendentals=36 * channels * TILE,
        ),
        name="pairs",
    )(info, in_hbm(preds[0]), *map(in_vmem, preds[1:]), target, area)


def join_kernel(left, right, out):
    out[:, :HALF] = left[:, TILE:]
    out[:, HALF:] = right[:, TILE:]


def join_tails(left, right):
    fixed = pl.BlockSpec(memory_space=pltpu.VMEM)
    return pl.pallas_call(
        join_kernel,
        in_specs=[fixed, fixed],
        out_specs=fixed,
        out_shape=pltpu.VMEM((left.shape[0], 2 * HALF), F32),
        compiler_params=pltpu.CompilerParams(vmem_limit_bytes=4 * MIB),
        name="join_tails",
    )(in_vmem(left), in_vmem(right))


def backward_kernel(info, *refs):
    near, own, side, relayed = refs[:4], refs[4], refs[5], refs[6:8]
    x_hbm, hidden, slope, ow, grad, away, keep, pg, x, up, out, sem = refs[8:]
    block, chunk = pl.program_id(0), pl.program_id(1)
    channels, each = pg.shape[0], grad.shape[0]
    wide, chunks = each * TILE, len(SLOTS) // each

    def fetch(i):
        tile = pl.ds(pl.multiple_of(info[1 + i] * TILE, TILE), TILE)
        place = slice(i * TILE, (i + 1) * TILE)
        return pltpu.make_async_copy(x_hbm.at[:, tile], x.at[:, place], sem.at[i])

    @pl.when((block == 0) & (chunk == 0))
    def _():
        for i in range(len(SLOTS)):
            fetch(i).start()
        for i, ref in enumerate((*near, own, side)):
            pg[:, i * TILE : (i + 1) * TILE] = ref[:, :TILE].astype(BF16)
        for i in range(len(FAR)):
            for k, ref in enumerate(relayed):
                low = (6 + i) * TILE + k * HALF
                pg[:, low : low + HALF] = ref[:, i * HALF : (i + 1) * HALF].astype(BF16)

    for c in range(chunks):

        @pl.when((block == 0) & (chunk == c))
        def _():
            for i in range(c * each, (c + 1) * each):
                fetch(i).wait()

    span = pl.ds(pl.multiple_of(chunk * wide, wide), wide)
    pgt = pg[:, span]
    own_rows = pl.ds(pl.multiple_of(block * BLOCK, BLOCK), BLOCK)
    for low in range(0, wide, ROWS):
        hg = mm(ow[...], pgt[:, low : low + ROWS], 1, 0)
        i, cols = low // TILE, slice(low % TILE, low % TILE + ROWS)
        factor = slope[chunk * each + i, own_rows, cols]
        grad[i, :, cols] = (hg * factor.astype(F32)).astype(BF16)
    acts = [hidden[chunk * each + i, own_rows, :] for i in range(each)]
    joined = jnp.concatenate([grad[i] for i in range(each)], axis=1)
    opening = chunk == 0
    part_out = mm(pgt, jnp.concatenate(acts, axis=1), 1, 1)
    out[:channels, :] = jnp.where(opening, 0.0, out[:channels, :]) + part_out
    part_up = mm(x[:, span], joined, 1, 1).reshape(up.shape)
    up[...] = jnp.where(opening, 0.0, up[...]) + part_up

    @pl.when(chunk == chunks - 1)
    def _():
        depth = keep.shape[2] - 128
        cols = pl.ds(pl.multiple_of(block * BLOCK, BLOCK), BLOCK)
        some = BLOCK // 16
        rows = pl.ds(block * some, some)
        for ref, core in ((keep, info[0]), (away, 1 - info[0])):
            ref[:, :, cols] = up[:, core]
        up[:some, :, :, :128] = out[...].T.reshape(some, 2, 8, 128)
        for ref, core in ((keep, info[0]), (away, 1 - info[0])):
            ref[rows, :, depth:] = up[:some, core, :, :128]


def backward(info, near, own, side, relayed, x, hidden, slope, ow):
    depth, cells = x.shape
    channels = ow.shape[1]
    chips, blocks = depth // 16, depth // BLOCK
    at = pl.BlockSpec((SPAN // TILE, BLOCK, TILE), lambda b, c, t: (c, b, 0))
    fixed = pl.BlockSpec(memory_space=pltpu.VMEM)
    return pl.pallas_call(
        backward_kernel,
        grid_spec=pltpu.PrefetchScalarGridSpec(
            num_scalar_prefetch=1,
            grid=(blocks, cells // SPAN),
            in_specs=[fixed] * 4
            + [pl.BlockSpec((channels, TILE), lambda b, c, t: (0, 0))]
            + [fixed] * 3
            + [
                pl.BlockSpec(memory_space=pl.ANY),
                fixed,
                fixed,
                pl.BlockSpec((BLOCK, channels), lambda b, c, t: (b, 0)),
            ],
            out_specs=[at, fixed, fixed],
            scratch_shapes=[
                pltpu.VMEM((channels, cells), BF16),
                pltpu.VMEM((depth, cells), BF16),
                pltpu.VMEM((chips, 2, 8, BLOCK), F32),
                pltpu.VMEM((128, BLOCK), F32),
                pltpu.SemaphoreType.DMA((len(SLOTS),)),
            ],
        ),
        out_shape=[pltpu.HBM(hidden.shape, BF16)]
        + [pltpu.VMEM((chips, 8, depth + 128), F32)] * 2,
        compiler_params=pltpu.CompilerParams(vmem_limit_bytes=28 * MIB),
        cost_estimate=pl.CostEstimate(
            flops=2 * depth * (depth + 2 * channels) * cells,
            bytes_accessed=8 * depth * cells + 4 * depth * depth,
            transcendentals=0,
        ),
        name="backward",
    )(
        info,
        *map(in_vmem, near),
        in_hbm(own),
        *map(in_vmem, (side, *relayed)),
        in_hbm(x),
        in_vmem(hidden),
        in_vmem(slope),
        in_hbm(ow),
    )


def feature_kernel(table, w, grad, out):
    out[0] = mm(w[...], grad[0], 1, 0).astype(BF16)


def feature_grad(table, w, grad):
    depth, cells = grad.shape[1], grad.shape[0] * TILE
    return pl.pallas_call(
        feature_kernel,
        grid_spec=pltpu.PrefetchScalarGridSpec(
            num_scalar_prefetch=1,
            grid=(cells // TILE,),
            in_specs=[
                pl.BlockSpec((depth, depth), lambda g, t: (0, 0)),
                pl.BlockSpec((1, depth, TILE), lambda g, t: (g, 0, 0)),
            ],
            out_specs=pl.BlockSpec((1, depth, TILE), lambda g, t: (0, 0, t[1 + g])),
        ),
        out_shape=jax.ShapeDtypeStruct((1, depth, cells), BF16),
        compiler_params=pltpu.CompilerParams(vmem_limit_bytes=24 * MIB),
        cost_estimate=pl.CostEstimate(
            flops=2 * depth * depth * cells,
            bytes_accessed=4 * depth * cells + 2 * depth * depth,
            transcendentals=0,
        ),
        name="feature_grad",
    )(table, in_hbm(w), in_hbm(grad))


def total_kernel(scale, parts, up, out):
    depth, channels = up.shape[1], out.shape[1]
    acc = parts[0]
    for c in range(1, parts.shape[0]):
        acc = acc + parts[c]
    acc = acc * scale
    up[...] = acc[:, :depth]
    out[...] = acc[:, depth : depth + channels]


def total(parts, depth, channels, scale):
    rows = parts.shape[1]
    return pl.pallas_call(
        functools.partial(total_kernel, scale),
        in_specs=[pl.BlockSpec(memory_space=pltpu.VMEM)],
        out_shape=[
            jax.ShapeDtypeStruct((rows, depth), F32),
            jax.ShapeDtypeStruct((rows, channels), F32),
        ],
        compiler_params=pltpu.CompilerParams(vmem_limit_bytes=16 * MIB),
        name="total",
    )(parts)


def spread(away, keep):
    swapped = lax.ppermute(away, "core", [(0, 1), (1, 0)])
    return lax.all_to_all(keep + swapped, CHIP, 0, 0, tiled=True)


def body(features, up_weight, out_weight, target, area):
    x = features[0]
    depth, cells = x.shape
    channels = out_weight.shape[1]
    owt = out_weight.T
    z, y = lax.axis_index("z"), lax.axis_index("ylo")
    core = lax.axis_index("core")

    tiles = {
        s: (2 * lax.rem(z + s[0], 4) + lax.bitwise_xor(y, s[1])).astype(jnp.int32) for s in SLOTS
    }
    info = [core.astype(jnp.int32)] + [tiles[s] for s in SLOTS + ORDER]
    info = jnp.stack(info + [jnp.int32(SLOTS.index(s)) for s in ORDER])

    def relay(blocks, step):
        return lax.ppermute(join_tails(*blocks), "z", [(i, (i + step) % 4) for i in range(4)])

    hidden, slope, *sent, wt, ow = forward(info, x, up_weight, owt)
    got = {}
    for s, p in zip(FIRST, sent):
        got[s] = lax.ppermute(p, MEMBER, route(s, False))
    hidden, slope, *sent = forward(info, x, wt, owt, (hidden, slope))
    for s, p in zip(SECOND, sent):
        got[s] = p if s == (0, 0) else lax.ppermute(p, MEMBER, route(s, False))
    order = SIDE + NEAR + FAR
    own, side, *sent = pairs(info, [got[s] for s in order], target, area[None, :])

    near = [lax.ppermute(block, MEMBER, route(s, True)) for s, block in zip(NEAR, sent)]
    side = lax.ppermute(side, MEMBER, route((0, 1), True))
    relayed = relay(near[0::2], -1), relay(near[1::2], 1)
    pre_grad, away, keep = backward(info, near, own, side, relayed, x, hidden, slope, ow)
    parts = spread(away, keep)
    fgrad = feature_grad(info, up_weight, pre_grad)
    scale = 1.0 / math.sqrt(cells * lax.axis_size(SPACE) * lax.axis_size(MEMBER))
    up_grad, out_grad = total(parts, depth, channels, scale)
    return fgrad, up_grad, out_grad


def solution(mesh):
    fine = Mesh(mesh.devices.reshape(4, 2, 4, 2, 2), DEVICE)
    in_specs = (P(MEMBER, None, SPACE), P(), P(), P(None, SPACE), P(SPACE))
    out_specs = (P(MEMBER, None, SPACE), P(DEVICE, None), P(DEVICE, None))
    return jax.shard_map(body, mesh=fine, in_specs=in_specs, out_specs=out_specs, check_vma=False)
```

```python
import functools
import math

import jax
import jax.numpy as jnp
from jax import lax
from jax.experimental import pallas as pl
from jax.experimental.pallas import tpu as pltpu
from jax.sharding import Mesh
from jax.sharding import PartitionSpec as P


MEMBER = ("z", "ylo")
CHIP = ("z", "ylo", "x", "yhi")
SPACE = ("x", "yhi", "core")
DEVICE = ("z", "ylo", "x", "yhi", "core")

NEAR = ((1, 0), (3, 0), (1, 1), (3, 1))
SIDE = ((0, 0), (0, 1))
FAR = ((2, 0), (2, 1))
SLOTS = NEAR + SIDE + FAR
GROUPS = (((2, 1), (2, 0)), ((1, 1), (3, 1), (0, 1)), ((1, 0), (3, 0), (0, 0)))
ORDER = GROUPS[0] + GROUPS[1] + GROUPS[2]

TILE = 512
SPAN = 1024
BLOCK = 512
HALF = 256
ROWS = 256
MIB = 1 << 20
BF16, F32 = jnp.bfloat16, jnp.float32


def route(slot, back):
    pairs = []
    for z in range(4):
        for y in range(2):
            here, there = 2 * z + y, 2 * ((z + slot[0]) % 4) + (y ^ slot[1])
            pairs.append((there, here) if back else (here, there))
    return pairs


def in_hbm(x):
    return pltpu.with_memory_space_constraint(x, pltpu.HBM)


def in_vmem(x):
    return pltpu.with_memory_space_constraint(x, pltpu.VMEM)


def smooth(diff):
    return diff * lax.rsqrt(diff * diff + 0.0625)


def mm(a, b, ca, cb):
    return lax.dot_general(a, b, (((ca,), (cb,)), ((), ())), preferred_element_type=F32)


def forward_kernel(first, base, info, *refs):
    if first:
        x, w, owt, hidden, slope, *preds, wt, ow = refs
    else:
        x, wt, owt, _, _, hidden, slope, *preds = refs
    step = pl.program_id(0)

    if first:

        @pl.when(step == 0)
        def _():
            for i in range(0, w.shape[0], ROWS):
                wt[:, i : i + ROWS] = (w[i : i + ROWS, :] * 0.5).T
            ow[...] = (owt[...] * 0.5).T

    slot = info[17 + base + step]
    h = mm(wt[...], x[...], 1, 0)
    u = jnp.tanh(h) + 1.0
    act = h * u
    rounded = act.astype(BF16)
    hidden[slot] = rounded
    slope[slot] = (u + act * (2.0 - u)).astype(BF16)
    pred = mm(owt[...], rounded, 1, 0)
    for i, out in enumerate(preds):

        @pl.when(step == i)
        def _():
            out[...] = pred


def forward(group, info, x, w, owt, carried=None):
    first = carried is None
    depth, _ = x.shape
    channels = owt.shape[0]
    n, base = len(GROUPS[group]), ORDER.index(GROUPS[group][0])
    at_tile = pl.BlockSpec((depth, TILE), lambda g, t: (0, t[9 + base + g]))
    whole = lambda *s: pl.BlockSpec(s, lambda g, t: (0,) * len(s))
    fixed = pl.BlockSpec(memory_space=pltpu.VMEM)
    act = pltpu.VMEM((len(SLOTS), depth, TILE), BF16)
    out_shape = [act, act] + [pltpu.VMEM((channels, TILE), F32)] * n
    out_specs = [fixed, fixed] + [fixed] * n
    w_spec = whole(depth, depth) if first else fixed
    w = in_hbm(w) if first else in_vmem(w)
    args, in_specs = [in_hbm(x), w, in_hbm(owt)], [at_tile, w_spec, whole(channels, depth)]
    alias = {}
    if first:
        out_shape += [pltpu.VMEM((depth, depth), BF16), pltpu.HBM((depth, channels), BF16)]
        out_specs += [fixed, whole(depth, channels)]
    else:
        if (0, 0) in GROUPS[group]:
            out_shape[-1] = pltpu.HBM((channels, TILE), F32)
            out_specs[-1] = whole(channels, TILE)
        args += map(in_vmem, carried)
        in_specs += [fixed, fixed]
        alias = {4: 0, 5: 1}
    return pl.pallas_call(
        functools.partial(forward_kernel, first, base),
        grid_spec=pltpu.PrefetchScalarGridSpec(
            num_scalar_prefetch=1, grid=(n,), in_specs=in_specs, out_specs=out_specs
        ),
        out_shape=out_shape,
        input_output_aliases=alias,
        compiler_params=pltpu.CompilerParams(vmem_limit_bytes=16 * MIB),
        cost_estimate=pl.CostEstimate(
            flops=2 * depth * (depth + channels) * TILE * n,
            bytes_accessed=6 * depth * TILE * n + 2 * depth * depth,
            transcendentals=depth * TILE * n,
        ),
        name="forward",
    )(info, *args)


def pair_kernel(info, *refs):
    preds, (target, area), outs = refs[:8], refs[8:10], refs[10:]
    own_out, side_out, *near_outs = outs
    members = len(SLOTS)
    across = 0.95 / (members * (members - 1))
    channels = target.shape[0]
    for lane in range(0, TILE, 128):
        cols = slice(lane, lane + 128)
        weight = area[:, cols]
        second = lane >= HALF
        at = lane % HALF
        tail = slice(TILE + at, TILE + at + 128)
        for low in range(0, channels, 8):
            rows = slice(low, min(low + 8, channels))
            p = [r[rows, cols] for r in preds]
            t = target[rows, cols].astype(F32)
            total = [None] * members
            for a in range(members):
                for b in range(a + 1, members):
                    s = smooth(p[a] - p[b])
                    total[a] = s if total[a] is None else total[a] + s
                    total[b] = -s if total[b] is None else total[b] - s
            for a in range(members):
                g = weight * (smooth(p[a] - t) * (1.0 / members) - across * total[a])
                g = g.astype(BF16).astype(F32)
                if a < 6:
                    outs[a][rows, cols] = g
                else:
                    near_outs[2 * (a - 6) + second][rows, tail] = g


def pairs(info, preds, target, area):
    channels = target.shape[0]
    me = 1 + SLOTS.index((0, 0))
    fixed = pl.BlockSpec(memory_space=pltpu.VMEM)
    whole = pl.BlockSpec((channels, TILE), lambda g, t: (0, 0))
    return pl.pallas_call(
        pair_kernel,
        grid_spec=pltpu.PrefetchScalarGridSpec(
            num_scalar_prefetch=1,
            grid=(1,),
            in_specs=[whole]
            + [fixed] * 7
            + [
                pl.BlockSpec((channels, TILE), lambda g, t: (0, t[me])),
                pl.BlockSpec((1, TILE), lambda g, t: (0, t[me])),
            ],
            out_specs=[whole] + [fixed] * 5,
        ),
        out_shape=[pltpu.HBM((channels, TILE), F32), pltpu.VMEM((channels, TILE), F32)]
        + [pltpu.VMEM((channels, TILE + HALF), F32)] * 4,
        compiler_params=pltpu.CompilerParams(vmem_limit_bytes=16 * MIB),
        cost_estimate=pl.CostEstimate(
            flops=36 * 6 * channels * TILE,
            bytes_accessed=64 * channels * TILE,
            transcendentals=36 * channels * TILE,
        ),
        name="pairs",
    )(info, in_hbm(preds[0]), *map(in_vmem, preds[1:]), target, area)


def join_kernel(left, right, out):
    out[:, :HALF] = left[:, TILE:]
    out[:, HALF:] = right[:, TILE:]


def join_tails(left, right):
    fixed = pl.BlockSpec(memory_space=pltpu.VMEM)
    return pl.pallas_call(
        join_kernel,
        in_specs=[fixed, fixed],
        out_specs=fixed,
        out_shape=pltpu.VMEM((left.shape[0], 2 * HALF), F32),
        compiler_params=pltpu.CompilerParams(vmem_limit_bytes=4 * MIB),
        name="join_tails",
    )(in_vmem(left), in_vmem(right))


def backward_kernel(info, *refs):
    near, own, side, relayed = refs[:4], refs[4], refs[5], refs[6:8]
    x_hbm, hidden, slope, ow, grad, away, keep, pg, x, up, out, sem = refs[8:]
    block, chunk = pl.program_id(0), pl.program_id(1)
    channels, each = pg.shape[0], grad.shape[0]
    wide, chunks = each * TILE, len(SLOTS) // each

    def fetch(i):
        tile = pl.ds(pl.multiple_of(info[1 + i] * TILE, TILE), TILE)
        place = slice(i * TILE, (i + 1) * TILE)
        return pltpu.make_async_copy(x_hbm.at[:, tile], x.at[:, place], sem.at[i])

    @pl.when((block == 0) & (chunk == 0))
    def _():
        for i in range(len(SLOTS)):
            fetch(i).start()
        for i, ref in enumerate((*near, own, side)):
            pg[:, i * TILE : (i + 1) * TILE] = ref[:, :TILE].astype(BF16)
        for i in range(len(FAR)):
            for k, ref in enumerate(relayed):
                low = (6 + i) * TILE + k * HALF
                pg[:, low : low + HALF] = ref[:, i * HALF : (i + 1) * HALF].astype(BF16)

    for c in range(chunks):

        @pl.when((block == 0) & (chunk == c))
        def _():
            for i in range(c * each, (c + 1) * each):
                fetch(i).wait()

    span = pl.ds(pl.multiple_of(chunk * wide, wide), wide)
    pgt = pg[:, span]
    own_rows = pl.ds(pl.multiple_of(block * BLOCK, BLOCK), BLOCK)
    for low in range(0, wide, ROWS):
        hg = mm(ow[...], pgt[:, low : low + ROWS], 1, 0)
        i, cols = low // TILE, slice(low % TILE, low % TILE + ROWS)
        factor = slope[chunk * each + i, own_rows, cols]
        grad[i, :, cols] = (hg * factor.astype(F32)).astype(BF16)
    acts = [hidden[chunk * each + i, own_rows, :] for i in range(each)]
    joined = jnp.concatenate([grad[i] for i in range(each)], axis=1)
    opening = chunk == 0
    part_out = mm(pgt, jnp.concatenate(acts, axis=1), 1, 1)
    out[:channels, :] = jnp.where(opening, 0.0, out[:channels, :]) + part_out
    part_up = mm(x[:, span], joined, 1, 1).reshape(up.shape)
    up[...] = jnp.where(opening, 0.0, up[...]) + part_up

    @pl.when(chunk == chunks - 1)
    def _():
        depth = keep.shape[2] - 128
        cols = pl.ds(pl.multiple_of(block * BLOCK, BLOCK), BLOCK)
        some = BLOCK // 16
        rows = pl.ds(block * some, some)
        for ref, core in ((keep, info[0]), (away, 1 - info[0])):
            ref[:, :, cols] = up[:, core]
        up[:some, :, :, :128] = out[...].T.reshape(some, 2, 8, 128)
        for ref, core in ((keep, info[0]), (away, 1 - info[0])):
            ref[rows, :, depth:] = up[:some, core, :, :128]


def backward(info, near, own, side, relayed, x, hidden, slope, ow):
    depth, cells = x.shape
    channels = ow.shape[1]
    chips, blocks = depth // 16, depth // BLOCK
    at = pl.BlockSpec((SPAN // TILE, BLOCK, TILE), lambda b, c, t: (c, b, 0))
    fixed = pl.BlockSpec(memory_space=pltpu.VMEM)
    return pl.pallas_call(
        backward_kernel,
        grid_spec=pltpu.PrefetchScalarGridSpec(
            num_scalar_prefetch=1,
            grid=(blocks, cells // SPAN),
            in_specs=[fixed] * 4
            + [pl.BlockSpec((channels, TILE), lambda b, c, t: (0, 0))]
            + [fixed] * 3
            + [
                pl.BlockSpec(memory_space=pl.ANY),
                fixed,
                fixed,
                pl.BlockSpec((BLOCK, channels), lambda b, c, t: (b, 0)),
            ],
            out_specs=[at, fixed, fixed],
            scratch_shapes=[
                pltpu.VMEM((channels, cells), BF16),
                pltpu.VMEM((depth, cells), BF16),
                pltpu.VMEM((chips, 2, 8, BLOCK), F32),
                pltpu.VMEM((128, BLOCK), F32),
                pltpu.SemaphoreType.DMA((len(SLOTS),)),
            ],
        ),
        out_shape=[pltpu.HBM(hidden.shape, BF16)]
        + [pltpu.VMEM((chips, 8, depth + 128), F32)] * 2,
        compiler_params=pltpu.CompilerParams(vmem_limit_bytes=28 * MIB),
        cost_estimate=pl.CostEstimate(
            flops=2 * depth * (depth + 2 * channels) * cells,
            bytes_accessed=8 * depth * cells + 4 * depth * depth,
            transcendentals=0,
        ),
        name="backward",
    )(
        info,
        *map(in_vmem, near),
        in_hbm(own),
        *map(in_vmem, (side, *relayed)),
        in_hbm(x),
        in_vmem(hidden),
        in_vmem(slope),
        in_hbm(ow),
    )


def feature_kernel(table, w, grad, out):
    out[0] = mm(w[...], grad[0], 1, 0).astype(BF16)


def feature_grad(table, w, grad):
    depth, cells = grad.shape[1], grad.shape[0] * TILE
    return pl.pallas_call(
        feature_kernel,
        grid_spec=pltpu.PrefetchScalarGridSpec(
            num_scalar_prefetch=1,
            grid=(cells // TILE,),
            in_specs=[
                pl.BlockSpec((depth, depth), lambda g, t: (0, 0)),
                pl.BlockSpec((1, depth, TILE), lambda g, t: (g, 0, 0)),
            ],
            out_specs=pl.BlockSpec((1, depth, TILE), lambda g, t: (0, 0, t[1 + g])),
        ),
        out_shape=jax.ShapeDtypeStruct((1, depth, cells), BF16),
        compiler_params=pltpu.CompilerParams(vmem_limit_bytes=24 * MIB),
        cost_estimate=pl.CostEstimate(
            flops=2 * depth * depth * cells,
            bytes_accessed=4 * depth * cells + 2 * depth * depth,
            transcendentals=0,
        ),
        name="feature_grad",
    )(table, in_hbm(w), in_hbm(grad))


def total_kernel(scale, parts, up, out):
    depth, channels = up.shape[1], out.shape[1]
    acc = parts[0]
    for c in range(1, parts.shape[0]):
        acc = acc + parts[c]
    acc = acc * scale
    up[...] = acc[:, :depth]
    out[...] = acc[:, depth : depth + channels]


def total(parts, depth, channels, scale):
    rows = parts.shape[1]
    return pl.pallas_call(
        functools.partial(total_kernel, scale),
        in_specs=[pl.BlockSpec(memory_space=pltpu.VMEM)],
        out_shape=[
            jax.ShapeDtypeStruct((rows, depth), F32),
            jax.ShapeDtypeStruct((rows, channels), F32),
        ],
        compiler_params=pltpu.CompilerParams(vmem_limit_bytes=16 * MIB),
        name="total",
    )(parts)


def spread(away, keep):
    swapped = lax.ppermute(away, "core", [(0, 1), (1, 0)])
    return lax.all_to_all(keep + swapped, CHIP, 0, 0, tiled=True)


def body(features, up_weight, out_weight, target, area):
    x = features[0]
    depth, cells = x.shape
    channels = out_weight.shape[1]
    owt = out_weight.T
    z, y = lax.axis_index("z"), lax.axis_index("ylo")
    core = lax.axis_index("core")

    tiles = {
        s: (2 * lax.rem(z + s[0], 4) + lax.bitwise_xor(y, s[1])).astype(jnp.int32) for s in SLOTS
    }
    info = [core.astype(jnp.int32)] + [tiles[s] for s in SLOTS + ORDER]
    info = jnp.stack(info + [jnp.int32(SLOTS.index(s)) for s in ORDER])

    def relay(blocks, step):
        return lax.ppermute(join_tails(*blocks), "z", [(i, (i + step) % 4) for i in range(4)])

    hidden, slope, *sent, wt, ow = forward(0, info, x, up_weight, owt)
    got = {}
    for group in (1, 2):
        for s, p in zip(GROUPS[group - 1], sent):
            got[s] = lax.ppermute(p, MEMBER, route(s, False))
        hidden, slope, *sent = forward(group, info, x, wt, owt, (hidden, slope))
    for s, p in zip(GROUPS[2], sent):
        got[s] = p if s == (0, 0) else lax.ppermute(p, MEMBER, route(s, False))
    order = SIDE + NEAR + FAR
    own, side, *sent = pairs(info, [got[s] for s in order], target, area[None, :])

    near = [lax.ppermute(block, MEMBER, route(s, True)) for s, block in zip(NEAR, sent)]
    side = lax.ppermute(side, MEMBER, route((0, 1), True))
    relayed = relay(near[0::2], -1), relay(near[1::2], 1)
    pre_grad, away, keep = backward(info, near, own, side, relayed, x, hidden, slope, ow)
    parts = spread(away, keep)
    fgrad = feature_grad(info, up_weight, pre_grad)
    scale = 1.0 / math.sqrt(cells * lax.axis_size(SPACE) * lax.axis_size(MEMBER))
    up_grad, out_grad = total(parts, depth, channels, scale)
    return fgrad, up_grad, out_grad


def solution(mesh):
    fine = Mesh(mesh.devices.reshape(4, 2, 4, 2, 2), DEVICE)
    in_specs = (P(MEMBER, None, SPACE), P(), P(), P(None, SPACE), P(SPACE))
    out_specs = (P(MEMBER, None, SPACE), P(DEVICE, None), P(DEVICE, None))
    return jax.shard_map(body, mesh=fine, in_specs=in_specs, out_specs=out_specs, check_vma=False)
```
